32 devices in a mesh: row: 4 (over y, core), col: 8 (over z, x).
Axes of the slice: x: 2, y: 2, z: 4, core: 2. Of those that a mesh axis runs over, the one named last changes fastest.
Arguments:
- left_image: bfloat16 [32, 1024], P('row', 'col'), may hold values from -6 to 6
- right_image: bfloat16 [32, 1024], P('row', 'col'), may hold values from -6 to 6
- first_weight: bfloat16 [32, 9], replicated, may hold values from -2 to 2
- second_weight: bfloat16 [32, 288], replicated, may hold values from -0.375 to 0.375
- third_weight: bfloat16 [32, 288], replicated, may hold values from -0.375 to 0.375
- tile_base: int32 [4, 8], P('row', 'col'), may hold values from 0 to 96, as said below
- tile_width: int32 [4, 8], P('row', 'col'), may hold values from 32 to 128
Outputs:
- aggregated: bfloat16 [32, 1024, 128], P('row', 'col')
The draws below stay inside these ranges and needn't reach their ends.
Inputs may be any that keep to these rules, and one draw needn't show every extreme that they name: In every tile tile_base + tile_width <= 128; one tile has tile_base 0 and tile_width 128, another has tile_base 128 - 128 // 4 and tile_width 128 // 4.
All inputs are finite; a program needn't handle non-finite values.
Results may differ from the reference program's by a relative error of at most 0.0045.
Values may be sent and summed in bfloat16 or wider, within the bound.
A program may use at most 64 MiB of HBM per device.

```python
import jax
import jax.numpy as jnp
from jax import lax

CH = 32
NDISP = 128
TR = 8
TC = 128
HEIGHT = 32
WIDTH = 1024
TILE_ROWS = 4
TILE_COLS = 8


def tile_pair(key):
    inner_key = jax.random.fold_in(key, 7)
    key_width, key_order, key_base = jax.random.split(inner_key, 3)
    count_all = TILE_ROWS * TILE_COLS
    widths = jax.random.randint(key_width, (count_all,), NDISP // 4, NDISP + 1)
    ordering = jax.random.permutation(key_order, count_all)
    widths = widths.at[ordering[0]].set(NDISP).at[ordering[1]].set(NDISP // 4)
    bases = jax.random.randint(key_base, (count_all,), 0, NDISP - widths + 1)
    bases = bases.at[ordering[0]].set(0).at[ordering[1]].set(NDISP - NDISP // 4)
    return (bases.reshape(TILE_ROWS, TILE_COLS).astype(jnp.int32), widths.reshape(TILE_ROWS, TILE_COLS).astype(jnp.int32))


def draw_tile_base(key, part):
    return tile_pair(key)[0]


def draw_tile_width(key, part):
    return tile_pair(key)[1]


def drawn_boxes(key):
    inner_key = jax.random.fold_in(key, 11)
    key_col, key_row = jax.random.split(inner_key)
    box_cols = WIDTH // 4
    box_rows = HEIGHT - HEIGHT // 4
    col_start = jax.random.randint(key_col, (2,), 0, WIDTH - box_cols + 1)
    row_start = jax.random.randint(key_row, (2,), HEIGHT // 16, HEIGHT // 8 + 1)
    return (col_start, row_start, box_cols, box_rows)


def image_with_boxes(key, salt):
    col_start, row_start, box_cols, box_rows = drawn_boxes(key)
    own_key = jax.random.fold_in(key, salt)
    key_tex, key_level = jax.random.split(own_key)
    texture = jnp.clip(jax.random.normal(key_tex, (HEIGHT, WIDTH), jnp.float32), -6.0, 6.0)
    levels = jax.random.uniform(key_level, (2,), jnp.float32, -1.5, 1.5)
    row_place = jnp.arange(HEIGHT)[:, None]
    col_place = jnp.arange(WIDTH)[None, :]
    picture = texture
    for box_num in range(2):
        inside = (row_place >= row_start[box_num]) & (row_place < row_start[box_num] + box_rows) & (col_place >= col_start[box_num]) & (col_place < col_start[box_num] + box_cols)
        picture = jnp.where(inside, levels[box_num], picture)
    return picture.astype(jnp.bfloat16)


def draw_left_image(key, part):
    return image_with_boxes(key, 21)


def draw_right_image(key, part):
    return image_with_boxes(key, 22)


def normal_values(key, extent, deviation, bound, kind=jnp.bfloat16):
    array = deviation * jax.random.normal(key, extent, jnp.float32)
    return jnp.clip(array, min=-bound, max=bound).astype(kind)


def setup_inputs(seed: int = 0) -> dict:
    streams_of = jax.random.split(jax.random.key(seed), 8)
    return {
        "left_image": draw_left_image(jax.random.fold_in(streams_of[7], 71), 0),
        "right_image": draw_right_image(jax.random.fold_in(streams_of[7], 71), 0),
        "first_weight": normal_values(streams_of[2], (CH, 9), 9 ** -0.5, 2.0),
        "second_weight": normal_values(streams_of[3], (CH, 9 * CH), (9 * CH) ** -0.5, 0.375),
        "third_weight": normal_values(streams_of[4], (CH, 9 * CH), (9 * CH) ** -0.5, 0.375),
        "tile_base": draw_tile_base(jax.random.fold_in(streams_of[7], 71), 0),
        "tile_width": draw_tile_width(jax.random.fold_in(streams_of[7], 71), 0),
    }


PENALTY_SMALL = 0.5
PENALTY_LARGE = 4.0
INVALID_COST = 2.0
BIG_VALUE = 1e+30

def conv_layer(current, weight, in_chan, rectify):
    kernel = weight.reshape(CH, 3, 3, in_chan).transpose(0, 3, 1, 2)
    result = lax.conv_general_dilated(current[None], kernel, (1, 1), ((1, 1), (1, 1)), dimension_numbers=('NCHW', 'OIHW', 'NCHW'), preferred_element_type=jnp.float32)[0]
    if rectify:
        result = jnp.maximum(result, 0.0)
    return result.astype(jnp.bfloat16)

def tower(gray_image, first_weight, second_weight, third_weight):
    current = conv_layer(gray_image[None], first_weight, 1, True)
    current = conv_layer(current, second_weight, CH, True)
    return conv_layer(current, third_weight, CH, False)

def feature_norm(features):
    return jnp.maximum(jnp.sqrt(lax.optimization_barrier(jnp.sum(jnp.square(features.astype(jnp.float32)), axis=0))), 1.0)

def path_step(previous, column_cost):
    lowest = lax.optimization_barrier(jnp.min(previous, axis=-1, keepdims=True))
    edge_fill = jnp.full(previous.shape[:-1] + (1,), BIG_VALUE, previous.dtype)
    upper_step = jnp.concatenate([previous[..., 1:], edge_fill], axis=-1)
    lower_step = jnp.concatenate([edge_fill, previous[..., :-1]], axis=-1)
    chosen = jnp.minimum(jnp.minimum(previous, jnp.minimum(upper_step, lower_step) + PENALTY_SMALL), lowest + PENALTY_LARGE)
    updated = column_cost.astype(previous.dtype) + chosen - lowest
    return (updated, updated)

def sweep(volume_major, backward):
    start_state = jnp.zeros(volume_major.shape[1:], jnp.float32)
    final_state, path_costs = lax.scan(path_step, start_state, volume_major, reverse=backward)
    return path_costs

def reference(left_image, right_image, first_weight, second_weight, third_weight, tile_base, tile_width):
    left_feat = tower(left_image, first_weight, second_weight, third_weight)
    right_feat = tower(right_image, first_weight, second_weight, third_weight)
    left_norm = feature_norm(left_feat)
    right_norm = feature_norm(right_feat)
    height_all, width_all = left_image.shape
    right_pad = jnp.concatenate([jnp.zeros((CH, height_all, NDISP), right_feat.dtype), right_feat], axis=2)
    norm_pad = jnp.concatenate([jnp.ones((height_all, NDISP), right_norm.dtype), right_norm], axis=1)
    base_map = jnp.repeat(jnp.repeat(tile_base, TR, axis=0), TC, axis=1)
    width_map = jnp.repeat(jnp.repeat(tile_width, TR, axis=0), TC, axis=1)
    left_wide = left_feat.astype(jnp.float32)

    def one_shift(shift_num):
        offset = (NDISP - shift_num).astype(jnp.int32)
        shifted = lax.dynamic_slice_in_dim(right_pad, offset, width_all, axis=2).astype(jnp.float32)
        shift_norm = lax.dynamic_slice_in_dim(norm_pad, offset, width_all, axis=1)
        cosine = lax.optimization_barrier(jnp.sum(left_wide * shifted, axis=0)) / (left_norm * shift_norm)
        in_range = (shift_num >= base_map) & (shift_num < base_map + width_map)
        return jnp.where(in_range, 1.0 - cosine, INVALID_COST).astype(jnp.bfloat16)
    volume = lax.map(one_shift, jnp.arange(NDISP, dtype=jnp.int32))
    volume = jnp.transpose(volume, (1, 2, 0))
    summed = sweep(volume, False)
    summed = summed + sweep(volume, True)
    columns_first = jnp.swapaxes(volume, 0, 1)
    summed = summed + jnp.swapaxes(sweep(columns_first, False), 0, 1)
    summed = summed + jnp.swapaxes(sweep(columns_first, True), 0, 1)
    return (summed * 0.25).astype(jnp.bfloat16)
```

```python
from functools import partial

import jax
import jax.numpy as jnp
from jax import lax
from jax.experimental import pallas as pl
from jax.experimental.pallas import tpu as pltpu
from jax.sharding import PartitionSpec as P

NDISP = 128
MESH = pl.DeviceIdType.MESH


PENALTY_SMALL = 0.5
PENALTY_LARGE = 4.0
INVALID_COST = 2.0
BIG_VALUE = 1e30


ROW_BLOCKS = 3
COL_BLOCKS = 4


def exchange_kernel(left_ref, right_ref, out_ref, own_ref, send_sem, recv_sem):
    cols, rows = lax.axis_size("col"), lax.axis_size("row")
    col, row = lax.axis_index("col"), lax.axis_index("row")
    barrier = pltpu.get_barrier_semaphore()
    moves = [
        (down, right)
        for down in (-1, 0, 1)
        for right in (-1, 0, 1, 2)
        if (down, right) != (0, 0)
    ]

    def exists(down, right):
        return (
            (row + down >= 0) & (row + down < rows) & (col + right >= 0) & (col + right < cols)
        )

    count = jnp.int32(0)
    for down, right in moves:

        @pl.when(exists(-down, -right))
        def _():
            pl.semaphore_signal(
                barrier,
                inc=1,
                device_id={"row": row - down, "col": col - right},
                device_id_type=MESH,
            )

        count = count + exists(down, right).astype(jnp.int32)
    for num, image in enumerate((left_ref, right_ref)):
        value = image[...].astype(jnp.float32)
        own_ref[num] = value
        out_ref[1, 2, num] = value
    pl.semaphore_wait(barrier, count)

    def copy_of(down, right):
        return pltpu.make_async_remote_copy(
            src_ref=own_ref,
            dst_ref=out_ref.at[1 - down, 2 - right],
            send_sem=send_sem.at[1 - down, 2 - right],
            recv_sem=recv_sem.at[1 - down, 2 - right],
            device_id={"row": row + down, "col": col + right},
            device_id_type=MESH,
        )

    for down, right in moves:

        @pl.when(exists(down, right))
        def _():
            copy_of(down, right).start()

        @pl.when(jnp.logical_not(exists(-down, -right)))
        def _():
            out_ref[1 - down, 2 - right] = jnp.zeros(own_ref.shape, jnp.float32)

    for down, right in moves:

        @pl.when(exists(-down, -right))
        def _():
            copy_of(down, right).wait_recv()

        @pl.when(exists(down, right))
        def _():
            copy_of(down, right).wait_send()


def exchange(left_image, right_image):
    pair = (2, *left_image.shape)
    return pl.pallas_call(
        exchange_kernel,
        out_shape=jax.ShapeDtypeStruct((ROW_BLOCKS, COL_BLOCKS, *pair), jnp.float32),
        in_specs=[pl.BlockSpec(memory_space=pltpu.VMEM)] * 2,
        out_specs=pl.BlockSpec(memory_space=pltpu.VMEM),
        scratch_shapes=[
            pltpu.VMEM(pair, jnp.float32),
            pltpu.SemaphoreType.DMA((ROW_BLOCKS, COL_BLOCKS)),
            pltpu.SemaphoreType.DMA((ROW_BLOCKS, COL_BLOCKS)),
        ],
        compiler_params=pltpu.CompilerParams(collective_id=1, has_side_effects=True),
        name="exchange",
    )(left_image, right_image)


def layer(source, weight, span, out_rows, rectify, inside):
    chans, length = source.shape
    stacked = jnp.concatenate(
        [pltpu.roll(source, 1, 1), source, pltpu.roll(source, length - 1, 1)], axis=0
    ).astype(jnp.bfloat16)
    result = jnp.zeros((weight.shape[0], out_rows * span), jnp.float32)
    for row_off in range(3):
        result = result + jnp.dot(
            weight[:, row_off * 3 * chans : (row_off + 1) * 3 * chans],
            stacked[:, row_off * span : (row_off + out_rows) * span],
            preferred_element_type=jnp.float32,
        )
    if rectify:
        result = jnp.maximum(result, 0.0)
    return jnp.where(inside, result, 0.0).astype(jnp.bfloat16).astype(jnp.float32)


def cost_kernel(
    tile_rows, tile_cols, place_ref, blocks_ref, first_ref, second_ref, third_ref, out_ref
):
    base, width = place_ref[0], place_ref[1]
    first_row, first_col = place_ref[2], place_ref[3]
    total_rows, total_cols = place_ref[4], place_ref[5]
    weights = (first_ref[...], second_ref[...], third_ref[...])

    def tower(image, blocks):
        span = len(blocks) * tile_cols
        lines = [
            jnp.concatenate([blocks_ref[0, j, image] for j in blocks], axis=1)[
                tile_rows - 3 : tile_rows
            ],
            jnp.concatenate([blocks_ref[1, j, image] for j in blocks], axis=1),
            jnp.concatenate([blocks_ref[2, j, image] for j in blocks], axis=1)[0:3],
        ]
        current = jnp.concatenate(
            [line[i : i + 1] for line in lines for i in range(line.shape[0])], axis=1
        )
        for num in range(3):
            out_rows = tile_rows + 4 - 2 * num
            index = lax.broadcasted_iota(jnp.int32, (1, out_rows * span), 1)
            row_place = first_row - 2 + num + index // span
            col_place = first_col + (blocks[0] - 2) * tile_cols + index % span
            inside = (
                (row_place >= 0)
                & (row_place < total_rows)
                & (col_place >= 0)
                & (col_place < total_cols)
            )
            current = layer(current, weights[num], span, out_rows, num < 2, inside)
        return current, span

    left, left_span = tower(0, (1, 2, 3))
    right, right_span = tower(1, (0, 1, 2, 3))
    ext = 2 * tile_cols
    flip = lax.broadcasted_iota(jnp.int32, (ext, ext), 0) + lax.broadcasted_iota(
        jnp.int32, (ext, ext), 1
    )
    flip = (flip == ext - 1).astype(jnp.float32).astype(jnp.bfloat16)
    shifts = lax.broadcasted_iota(jnp.int32, (tile_cols, NDISP), 1)
    in_range = (shifts >= base) & (shifts < base + width)
    for y in range(tile_rows):
        own = left[:, y * left_span + tile_cols : y * left_span + 2 * tile_cols].T
        other = right[:, y * right_span + tile_cols : y * right_span + 3 * tile_cols]
        other = jnp.dot(other.astype(jnp.bfloat16), flip, preferred_element_type=jnp.float32)
        own_norm = jnp.maximum(jnp.sqrt(jnp.sum(own * own, axis=1, keepdims=True)), 1.0)
        other_norm = jnp.maximum(jnp.sqrt(jnp.sum(other * other, axis=0, keepdims=True)), 1.0)
        products = jnp.dot(
            own.astype(jnp.bfloat16),
            other.astype(jnp.bfloat16),
            preferred_element_type=jnp.float32,
        )
        cosine = products / (own_norm * other_norm)
        cosine = pltpu.roll(cosine, ext - tile_cols + 1, 1, stride=1, stride_axis=0)
        out_ref[y] = jnp.where(in_range, 1.0 - cosine[:, :NDISP], INVALID_COST).astype(
            jnp.bfloat16
        )


def cost_volume(place, blocks, weights):
    tile_rows, tile_cols = blocks.shape[3:]
    return pl.pallas_call(
        partial(cost_kernel, tile_rows, tile_cols),
        out_shape=jax.ShapeDtypeStruct((tile_rows, tile_cols, NDISP), jnp.bfloat16),
        in_specs=[pl.BlockSpec(memory_space=pltpu.SMEM)]
        + [pl.BlockSpec(memory_space=pltpu.VMEM)] * 4,
        out_specs=pl.BlockSpec(memory_space=pltpu.VMEM),
        compiler_params=pltpu.CompilerParams(vmem_limit_bytes=32 << 20),
        name="costs",
    )(place, blocks, *weights)


def mesh_barrier(col, cols, row, rows):
    barrier = pltpu.get_barrier_semaphore()
    count = jnp.int32(0)
    for axis, place, size in (("col", col, cols), ("row", row, rows)):
        for step in (-1, 1):
            there = (place + step >= 0) & (place + step < size)

            @pl.when(there)
            def _():
                pl.semaphore_signal(
                    barrier, inc=1, device_id={axis: place + step}, device_id_type=MESH
                )

            count = count + there.astype(jnp.int32)
    return barrier, count


SUBS = 8
LEADS = NDISP // SUBS


def least(values):
    values = list(values)
    while len(values) > 1:
        pairs = [jnp.minimum(values[i], values[i + 1]) for i in range(0, len(values) - 1, 2)]
        values = pairs + ([values[-1]] if len(values) % 2 else [])
    return values[0]


def split(value):
    high = value.astype(jnp.bfloat16)
    rest = value - high.astype(jnp.float32)
    mid = rest.astype(jnp.bfloat16)
    low = (rest - mid.astype(jnp.float32)).astype(jnp.bfloat16)
    return high, mid, low


def path_kernel(
    tile_rows,
    tile_cols,
    volume_ref,
    out_ref,
    by_col,
    v_cost,
    h_cost,
    h_path,
    v_path,
    total,
    local,
    reach,
    landed,
    entry,
    h_send,
    h_recv,
    v_send,
    v_recv,
    h_send_sem,
    h_recv_sem,
    v_send_sem,
    v_recv_sem,
):
    cols, rows = lax.axis_size("col"), lax.axis_size("row")
    col, row = lax.axis_index("col"), lax.axis_index("row")
    barrier, count = mesh_barrier(col, cols, row, rows)
    blocks = NDISP // tile_rows
    steps = tile_cols // blocks
    vreg = (SUBS, NDISP)
    sub = lax.broadcasted_iota(jnp.int32, vreg, 0)
    lane = lax.broadcasted_iota(jnp.int32, vreg, 1)
    first_edge = jnp.where(sub == 0, BIG_VALUE, PENALTY_SMALL)
    last_edge = jnp.where(sub == SUBS - 1, BIG_VALUE, PENALTY_SMALL)
    near_row = lax.broadcasted_iota(jnp.int32, (NDISP, NDISP), 0)
    near_col = lax.broadcasted_iota(jnp.int32, (NDISP, NDISP), 1)
    order = ((near_row % SUBS) * LEADS + near_row // SUBS == near_col).astype(jnp.float32)
    order = order.astype(jnp.bfloat16)

    def ordered(block):
        return lax.dot_general(
            order, block, (((1,), (1,)), ((), ())), preferred_element_type=jnp.float32
        )

    def restored(block, parts):
        turned = block.T
        return sum(
            jnp.dot(part, order, preferred_element_type=jnp.float32)
            for part in split(turned)[:parts]
        )

    def put(ref, where, block):
        for lead in range(LEADS):
            ref[(*where, lead)] = block[lead * SUBS : lead * SUBS + SUBS]

    def prepare(y, carried):
        block = volume_ref[y]
        by_col[:, y, :] = block.astype(jnp.float32)
        put(v_cost, (y,), ordered(block))
        return carried

    for y in range(tile_rows):
        prepare(y, 0)

    def turn(step, carried):
        block = by_col[pl.ds(step, blocks, stride=steps)].reshape(NDISP, NDISP)
        put(h_cost, (step,), ordered(block.astype(jnp.bfloat16)))
        return carried

    for step in range(steps):
        turn(step, 0)
    pl.semaphore_wait(barrier, count)

    def advance(state, here):
        lowest = least(state)
        lowest = jnp.minimum(lowest, pltpu.roll(lowest, 4, 0))
        turned = [pltpu.roll(lowest, shift, 0) for shift in (1, 2, 3)]
        lowest = jnp.minimum(
            jnp.minimum(lowest, turned[0]), jnp.minimum(turned[1], turned[2])
        )
        jump = lowest + PENALTY_LARGE
        below = pltpu.roll(state[LEADS - 1], 1, 0) + first_edge
        above = pltpu.roll(state[0], SUBS - 1, 0) + last_edge
        ext = [below, *(value + PENALTY_SMALL for value in state), above]
        new = []
        for lead in range(LEADS):
            near = jnp.minimum(state[lead], jnp.minimum(ext[lead], ext[lead + 2]))
            new.append(jnp.minimum(near, jump) + here[lead])
        return tuple(new), lowest

    def transfer(way, backward):
        def one_block(block, carried):
            reached = {0: jnp.zeros(vreg, jnp.float32)}
            for step in range(steps):
                place = block * steps + jnp.where(backward, steps - 1 - step, step)
                here = by_col[place]
                after = {}
                for off in range(-step - 1, step + 2):
                    cost = here
                    if off:
                        inside = lane < NDISP - off if off > 0 else lane >= -off
                        cost = jnp.where(inside, pltpu.roll(here, -off % NDISP, 1), BIG_VALUE)
                    side = [reached[o] for o in (off - 1, off + 1) if o in reached]
                    near = least(side) + PENALTY_SMALL if side else None
                    if off in reached:
                        near = reached[off] if near is None else jnp.minimum(reached[off], near)
                    after[off] = near + cost
                reached = after
                if step < steps - 1:
                    reach[way, block, step] = least(reached.values())
            for off, value in reached.items():
                local[way, block, off + steps] = value
            return carried

        lax.fori_loop(0, blocks, one_block, 0, unroll=2)

        def load(step):
            step = jnp.where(backward, steps - 1 - step, step)
            return tuple(h_cost[step, lead] for lead in range(LEADS))

        for start in range(0, steps, 2):
            states = [load(start)]
            for step in range(start + 1, steps):
                here = load(step)
                states = [advance(state, here)[0] for state in states]
                if step == start + 1:
                    states.append(here)
            for num, state in enumerate(states):
                block = restored(jnp.concatenate(state, axis=0), 3) + PENALTY_LARGE
                landed[way, :, start + num] = block.reshape(blocks, *vreg)

    def run(axis, place, size, backward, send, recv, send_sem, recv_sem, sweep):
        way = backward.astype(jnp.int32)
        step = 1 - 2 * way
        has_source = (place - step >= 0) & (place - step < size)
        has_target = (place + step >= 0) & (place + step < size)
        copy = pltpu.make_async_remote_copy(
            src_ref=send.at[way],
            dst_ref=recv.at[way],
            send_sem=send_sem.at[way],
            recv_sem=recv_sem.at[way],
            device_id={axis: place + step},
            device_id_type=MESH,
        )

        @pl.when(has_source)
        def _():
            copy.wait_recv()

        @pl.when(jnp.logical_not(has_source))
        def _():
            recv[way] = jnp.zeros(recv.shape[1:], jnp.float32)

        sweep(way, backward)

        @pl.when(has_target)
        def _():
            copy.start()

        return copy, has_target

    def row_sweep(way, backward):
        def body(index, state):
            block = jnp.where(backward, blocks - 1 - index, index)
            entry[way, block] = state
            lows = [jnp.min(state, axis=1, keepdims=True)]
            for step in range(steps - 1):
                lows.append(jnp.min(state + reach[way, block, step], axis=1, keepdims=True))
            best = state + local[way, block, steps]
            for step in range(steps):
                best = jnp.minimum(best, landed[way, block, step] + lows[step])
            for off in range(1, steps + 1):
                for o in (off, -off):
                    moved = pltpu.roll(state + local[way, block, o + steps], o % NDISP, 1)
                    best = jnp.minimum(best, moved)
            return best - lows[0]

        h_send[way] = lax.fori_loop(0, blocks, body, h_recv[way])

    def column_sweep(way, backward):
        state = tuple(v_recv[way, lead] for lead in range(LEADS))

        def body(index, state):
            place = jnp.where(backward, tile_rows - 1 - index, index)
            here = [v_cost[place, lead] for lead in range(LEADS)]
            state, lowest = advance(state, here)
            for lead in range(LEADS):
                v_path[way, place, lead] = state[lead] - lowest
            return tuple(value - lowest for value in state)

        state = lax.fori_loop(0, tile_rows, body, state)
        for lead in range(LEADS):
            v_send[way, lead] = state[lead]

    right_half = col > cols - 1 - col

    def horizontal(turn):
        backward = right_half if turn == 0 else jnp.logical_not(right_half)
        return run(
            "col", col, cols, backward, h_send, h_recv, h_send_sem, h_recv_sem, row_sweep
        )

    def prepared(turn):
        backward = right_half if turn == 0 else jnp.logical_not(right_half)
        transfer(backward.astype(jnp.int32), backward)

    def vertical():
        def one(turn, carried):
            lower_half = row > rows - 1 - row
            backward = lower_half != (turn == 1)
            copy, sent = run(
                "row", row, rows, backward, v_send, v_recv, v_send_sem, v_recv_sem, column_sweep
            )

            @pl.when(sent)
            def _():
                copy.wait_send()

            return carried

        lax.fori_loop(0, 2, one, 0)

        def gather_row(y, carried):
            block = jnp.concatenate(
                [v_path[0, y, lead] + v_path[1, y, lead] for lead in range(LEADS)], axis=0
            )
            total[:, y, :] = restored(block, 2)
            return carried

        for y in range(tile_rows):
            gather_row(y, 0)

    early = 2 * jnp.minimum(col, cols - 1 - col) < cols // 2

    prepared(0)
    first, first_sent = horizontal(0)
    prepared(1)

    @pl.when(early)
    def _():
        vertical()

    second, second_sent = horizontal(1)

    @pl.when(jnp.logical_not(early))
    def _():
        vertical()

    states = []
    for way in range(2):
        block = entry[way].reshape(NDISP, NDISP)
        block = sum(ordered(part) for part in split(block))
        states.append(tuple(block[lead * SUBS : lead * SUBS + SUBS] for lead in range(LEADS)))

    def dense(index, states):
        after = []
        for way, state in enumerate(states):
            place = steps - 1 - index if way else index
            state, lowest = advance(state, [h_cost[place, lead] for lead in range(LEADS)])
            state = tuple(value - lowest for value in state)
            for lead in range(LEADS):
                h_path[way, place, lead] = state[lead]
            after.append(state)
        return tuple(after)

    lax.fori_loop(0, steps, dense, tuple(states))

    for step in range(steps):
        block = jnp.concatenate(
            [h_path[0, step, lead] + h_path[1, step, lead] for lead in range(LEADS)], axis=0
        )
        where = pl.ds(step, blocks, stride=steps)
        total[where] = (total[where] + restored(block, 2).reshape(blocks, *vreg)) * 0.25
    for y in range(tile_rows):
        out_ref[y] = total[:, y, :].astype(jnp.bfloat16)

    @pl.when(first_sent)
    def _():
        first.wait_send()

    @pl.when(second_sent)
    def _():
        second.wait_send()


def aggregate(volume):
    tile_rows, tile_cols, disps = volume.shape
    vregs = (LEADS, SUBS, NDISP)
    vreg = (SUBS, NDISP)
    blocks = NDISP // tile_rows
    steps = tile_cols // blocks
    return pl.pallas_call(
        partial(path_kernel, tile_rows, tile_cols),
        out_shape=jax.ShapeDtypeStruct(volume.shape, jnp.bfloat16),
        in_specs=[pl.BlockSpec(memory_space=pltpu.VMEM)],
        out_specs=pl.BlockSpec(memory_space=pltpu.VMEM),
        scratch_shapes=[
            pltpu.VMEM((tile_cols, tile_rows, NDISP), jnp.float32),
            pltpu.VMEM((tile_rows, *vregs), jnp.float32),
            pltpu.VMEM((steps, *vregs), jnp.float32),
            pltpu.VMEM((2, steps, *vregs), jnp.float32),
            pltpu.VMEM((2, tile_rows, *vregs), jnp.float32),
            pltpu.VMEM((tile_cols, tile_rows, NDISP), jnp.float32),
            pltpu.VMEM((2, blocks, 2 * steps + 1, *vreg), jnp.float32),
            pltpu.VMEM((2, blocks, steps - 1, *vreg), jnp.float32),
            pltpu.VMEM((2, blocks, steps, *vreg), jnp.float32),
            pltpu.VMEM((2, blocks, *vreg), jnp.float32),
            pltpu.VMEM((2, *vreg), jnp.float32),
            pltpu.VMEM((2, *vreg), jnp.float32),
            pltpu.VMEM((2, *vregs), jnp.float32),
            pltpu.VMEM((2, *vregs), jnp.float32),
            pltpu.SemaphoreType.DMA((2,)),
            pltpu.SemaphoreType.DMA((2,)),
            pltpu.SemaphoreType.DMA((2,)),
            pltpu.SemaphoreType.DMA((2,)),
        ],
        compiler_params=pltpu.CompilerParams(
            collective_id=0, has_side_effects=True, vmem_limit_bytes=48 << 20
        ),
        name="paths",
    )(volume)


def on_device(
    left_image, right_image, first_weight, second_weight, third_weight, tile_base, tile_width
):
    weights = (first_weight, second_weight, third_weight)
    tile_rows, tile_cols = left_image.shape
    rows, cols = lax.axis_size("row"), lax.axis_size("col")
    blocks = exchange(left_image, right_image)
    place = jnp.stack(
        [
            tile_base[0, 0],
            tile_width[0, 0],
            lax.axis_index("row") * tile_rows,
            lax.axis_index("col") * tile_cols,
            jnp.int32(rows * tile_rows),
            jnp.int32(cols * tile_cols),
        ]
    )
    return aggregate(cost_volume(place, blocks, weights))


def solution(mesh):
    placed = (P("row", "col"), P("row", "col"), P(), P(), P(), P("row", "col"), P("row", "col"))
    return jax.shard_map(
        on_device, mesh=mesh, in_specs=placed, out_specs=P("row", "col", None), check_vma=False
    )
```

```python
from functools import partial

import jax
import jax.numpy as jnp
from jax import lax
from jax.experimental import pallas as pl
from jax.experimental.pallas import tpu as pltpu
from jax.sharding import PartitionSpec as P

NDISP = 128
MESH = pl.DeviceIdType.MESH


PENALTY_SMALL = 0.5
PENALTY_LARGE = 4.0
INVALID_COST = 2.0
BIG_VALUE = 1e30

RIM = 3
SUBS = 8
LEADS = NDISP // SUBS
STEPS = 16
FIELDS = 4


def least(values):
    values = list(values)
    while len(values) > 1:
        pairs = [jnp.minimum(values[i], values[i + 1]) for i in range(0, len(values) - 1, 2)]
        values = pairs + ([values[-1]] if len(values) % 2 else [])
    return values[0]


def split(value):
    high = value.astype(jnp.bfloat16)
    rest = value - high.astype(jnp.float32)
    mid = rest.astype(jnp.bfloat16)
    low = (rest - mid.astype(jnp.float32)).astype(jnp.bfloat16)
    return high, mid, low


def owned(col, cols, tile_rows):
    return col // (cols // tile_rows)


def layer(source, weight, span, out_rows, rectify, inside):
    chans, length = source.shape
    stacked = jnp.concatenate(
        [pltpu.roll(source, 1, 1), source, pltpu.roll(source, length - 1, 1)], axis=0
    ).astype(jnp.bfloat16)
    result = jnp.zeros((weight.shape[0], out_rows * span), jnp.float32)
    for row_off in range(3):
        result = result + jnp.dot(
            weight[:, row_off * 3 * chans : (row_off + 1) * 3 * chans],
            stacked[:, row_off * span : (row_off + out_rows) * span],
            preferred_element_type=jnp.float32,
        )
    if rectify:
        result = jnp.maximum(result, 0.0)
    return (result * inside).astype(jnp.bfloat16).astype(jnp.float32)


def path_kernel(
    tile_rows,
    tile_cols,
    base_ref,
    width_ref,
    left_hbm,
    right_hbm,
    first_hbm,
    second_hbm,
    third_hbm,
    out_ref,
    left_ref,
    right_ref,
    first_ref,
    second_ref,
    third_ref,
    own_ref,
    gathered,
    lines,
    by_col,
    by_tile,
    volume,
    wide,
    v_cost,
    h_cost,
    t_cost,
    v_path,
    h_path,
    turned,
    total,
    local,
    reach,
    landed,
    entry_out,
    entry_in,
    v_send,
    v_recv,
    image_send_sem,
    image_recv_sem,
    volume_send_sem,
    volume_recv_sem,
    entry_send_sem,
    entry_recv_sem,
    v_send_sem,
    v_recv_sem,
    load_sem,
):
    cols, rows = lax.axis_size("col"), lax.axis_size("row")
    col, row = lax.axis_index("col"), lax.axis_index("row")
    share = cols // tile_rows
    line = owned(col, cols, tile_rows)
    leads = lax.rem(col, share) == 0
    blocks = tile_cols // STEPS
    groups = cols // SUBS
    vreg = (SUBS, NDISP)
    half = blocks * SUBS
    barrier = pltpu.get_barrier_semaphore()
    loads = [
        pltpu.make_async_copy(source, target, load_sem.at[num])
        for num, (source, target) in enumerate(
            (
                (left_hbm, left_ref),
                (right_hbm, right_ref),
                (first_hbm, first_ref),
                (second_hbm, second_ref),
                (third_hbm, third_ref),
            )
        )
    ]
    for load in loads:
        load.start()
    far = sorted(range(cols), key=lambda k: -min(k, cols - k))
    moves = [(down, lax.rem(col + k, cols), k) for down in (0, -1, 1) for k in far if k or down]

    def wanted(down, target):
        line = owned(target, cols, tile_rows)
        if down == 0:
            return jnp.bool_(True)
        return line < RIM if down > 0 else line >= tile_rows - RIM

    def sends(down, target):
        return wanted(down, target) & (row + down >= 0) & (row + down < rows)

    def receives(down):
        return wanted(down, col) & (row - down >= 0) & (row - down < rows)

    count = jnp.int32(0)
    for step in (-1, 1):
        there = (row + step >= 0) & (row + step < rows)

        @pl.when(there)
        def _():
            pl.semaphore_signal(
                barrier, inc=1, device_id={"row": row + step}, device_id_type=MESH
            )

        count = count + there.astype(jnp.int32)
    for down, other, k in moves:

        @pl.when(receives(down))
        def _():
            pl.semaphore_signal(
                barrier,
                inc=1,
                device_id={"row": row - down, "col": other},
                device_id_type=MESH,
            )

        count = count + sends(down, other).astype(jnp.int32)
    loads[0].wait()
    loads[1].wait()
    fields = [
        left_ref[...].astype(jnp.float32),
        right_ref[...].astype(jnp.float32),
        jnp.full(left_ref.shape, base_ref[0, 0].astype(jnp.float32)),
        jnp.full(left_ref.shape, width_ref[0, 0].astype(jnp.float32)),
    ]
    value = jnp.concatenate(fields, axis=0).astype(jnp.bfloat16)
    own_ref[...] = value
    for down in (-1, 1):

        @pl.when(jnp.logical_not(receives(down)))
        def _():
            gathered[1 - down] = jnp.zeros(gathered.shape[1:], jnp.bfloat16)

    gathered[1, col] = value
    pl.semaphore_wait(barrier, count)

    def image_copy(down, target, source, slot):
        return pltpu.make_async_remote_copy(
            src_ref=own_ref,
            dst_ref=gathered.at[1 - down, source],
            send_sem=image_send_sem.at[1 - down, slot],
            recv_sem=image_recv_sem.at[1 - down, source],
            device_id={"row": row + down, "col": target},
            device_id_type=MESH,
        )

    for down, other, k in moves:

        @pl.when(sends(down, other))
        def _():
            image_copy(down, other, col, k).start()

    for down, other, k in moves:

        @pl.when(receives(down))
        def _():
            image_copy(down, other, other, k).wait_recv()

    def volume_copy(tile, y, slot):
        return pltpu.make_async_remote_copy(
            src_ref=by_tile.at[tile],
            dst_ref=volume.at[y],
            send_sem=volume_send_sem.at[tile],
            recv_sem=volume_recv_sem.at[y],
            device_id={"col": slot},
            device_id_type=MESH,
        )

    for load in loads[2:]:
        load.wait()
    weights = (first_ref[...].astype(jnp.float32).T.astype(jnp.bfloat16), second_ref[...], third_ref[...])
    span = (cols + 1) * tile_cols
    column = lax.broadcasted_iota(jnp.int32, (1, span), 1)
    for down in range(3):
        for other in range(cols):
            pair = gathered[down, other, : 2 * tile_rows].astype(jnp.float32)
            for image in range(2):
                lines[
                    image,
                    down * tile_rows : (down + 1) * tile_rows,
                    other * tile_cols : (other + 1) * tile_cols,
                ] = pair[image * tile_rows : (image + 1) * tile_rows]
    lines[:, :, cols * tile_cols :] = jnp.zeros((2, 3 * tile_rows, tile_cols), jnp.float32)

    def tower(image):
        current = jnp.concatenate(
            [
                lines[image, pl.ds(tile_rows + line - RIM + i, 1), :]
                for i in range(2 * RIM + 1)
            ],
            axis=1,
        )
        for num in range(RIM):
            edge = RIM - 1 - num
            inside = []
            for i in range(-edge, edge + 1):
                place = row * tile_rows + line + i
                limit = jnp.where((place >= 0) & (place < rows * tile_rows), cols * tile_cols, 0)
                inside.append(jnp.where(column < limit, 1.0, 0.0))
            inside = jnp.concatenate(inside, axis=1)
            current = layer(current, weights[num], span, 2 * edge + 1, num < RIM - 1, inside)
        return current

    left = tower(0)
    right = tower(1)
    ext = 2 * tile_cols
    flip = lax.broadcasted_iota(jnp.int32, (ext, ext), 0) + lax.broadcasted_iota(
        jnp.int32, (ext, ext), 1
    )
    flip = (flip == ext - 1).astype(jnp.float32).astype(jnp.bfloat16)
    shifts = lax.broadcasted_iota(jnp.int32, (tile_cols, NDISP), 1).astype(jnp.float32)
    for tile in range(cols):
        begin = tile * tile_cols
        own = left[:, begin : begin + tile_cols].T
        before = (begin or span) - tile_cols
        other = jnp.concatenate(
            [right[:, before : before + tile_cols], right[:, begin : begin + tile_cols]], axis=1
        )
        other = jnp.dot(other.astype(jnp.bfloat16), flip, preferred_element_type=jnp.float32)
        own_norm = jnp.maximum(jnp.sqrt(jnp.sum(own * own, axis=1, keepdims=True)), 1.0)
        other_norm = jnp.maximum(jnp.sqrt(jnp.sum(other * other, axis=0, keepdims=True)), 1.0)
        products = jnp.dot(
            own.astype(jnp.bfloat16),
            other.astype(jnp.bfloat16),
            preferred_element_type=jnp.float32,
        )
        cosine = products / (own_norm * other_norm)
        cosine = pltpu.roll(cosine, ext - tile_cols + 1, 1, stride=1, stride_axis=0)
        extent = gathered[1, tile, 2 * tile_rows :].astype(jnp.float32)
        base, width = extent[0:1], extent[tile_rows : tile_rows + 1]
        in_range = (shifts >= base) & (shifts < base + width)
        cost = jnp.where(in_range, 1.0 - cosine[:, :NDISP], INVALID_COST).astype(jnp.bfloat16)
        by_tile[tile] = cost
        by_col[tile // SUBS, :, tile % SUBS, :] = cost.astype(jnp.float32)

        @pl.when(leads & (col != tile))
        def _():
            volume_copy(tile, line, tile).start()

        @pl.when(leads & (col == tile))
        def _():
            volume[line] = by_tile[tile]

    sub = lax.broadcasted_iota(jnp.int32, vreg, 0)
    lane = lax.broadcasted_iota(jnp.int32, vreg, 1)
    first_edge = jnp.where(sub == 0, BIG_VALUE, PENALTY_SMALL)
    last_edge = jnp.where(sub == SUBS - 1, BIG_VALUE, PENALTY_SMALL)
    near_row = lax.broadcasted_iota(jnp.int32, (NDISP, NDISP), 0)
    near_col = lax.broadcasted_iota(jnp.int32, (NDISP, NDISP), 1)
    order = ((near_row % SUBS) * LEADS + near_row // SUBS == near_col).astype(jnp.float32)
    order = order.astype(jnp.bfloat16)
    same = (near_row == near_col).astype(jnp.float32).astype(jnp.bfloat16)

    def ordered(block):
        return lax.dot_general(
            order, block, (((1,), (1,)), ((), ())), preferred_element_type=jnp.float32
        )

    def upright(block, parts):
        return sum(
            lax.dot_general(
                same, part, (((1,), (1,)), ((), ())), preferred_element_type=jnp.float32
            )
            for part in split(block)[:parts]
        )

    def lay(ref, where, state):
        for lead in range(LEADS):
            ref[(*where, pl.ds(lead, SUBS, stride=LEADS), slice(None))] = state[lead]

    def put(ref, where, block):
        for lead in range(LEADS):
            ref[(*where, lead)] = block[lead * SUBS : lead * SUBS + SUBS]

    def take(ref, *where):
        return tuple(ref[(*where, lead)] for lead in range(LEADS))

    def advance(state, here):
        lowest = least(state)
        lowest = jnp.minimum(lowest, pltpu.roll(lowest, 4, 0))
        turned = [pltpu.roll(lowest, shift, 0) for shift in (1, 2, 3)]
        lowest = jnp.minimum(
            jnp.minimum(lowest, turned[0]), jnp.minimum(turned[1], turned[2])
        )
        jump = lowest + PENALTY_LARGE
        below = pltpu.roll(state[LEADS - 1], 1, 0) + first_edge
        above = pltpu.roll(state[0], SUBS - 1, 0) + last_edge
        ext = [below, *(value + PENALTY_SMALL for value in state), above]
        new = []
        for lead in range(LEADS):
            near = jnp.minimum(state[lead], jnp.minimum(ext[lead], ext[lead + 2]))
            new.append(jnp.minimum(near, jump) + here[lead])
        return tuple(new), lowest

    def slot_of(off):
        return 2 * STEPS if off == 0 else off + STEPS - (off > 0)

    def transfer(group, block):
        for way in range(2):
            reached = {0: jnp.zeros(vreg, jnp.float32)}
            reach[way, group, block, 0] = reached[0]
            for step in range(STEPS):
                here = by_col[group, block * STEPS + (STEPS - 1 - step if way else step)]
                after = {}
                for off in range(-step - 1, step + 2):
                    cost = here
                    if off:
                        inside = lane < NDISP - off if off > 0 else lane >= -off
                        cost = jnp.where(inside, pltpu.roll(here, -off % NDISP, 1), BIG_VALUE)
                    side = [reached[o] for o in (off - 1, off + 1) if o in reached]
                    near = least(side) + PENALTY_SMALL if side else None
                    if off in reached:
                        near = reached[off] if near is None else jnp.minimum(reached[off], near)
                    after[off] = near + cost
                reached = after
                if step < STEPS - 1:
                    reach[way, group, block, step + 1] = least(reached.values())
            for off, value in reached.items():
                local[way, group, block, slot_of(off)] = value

    def landings(group):
        def turn(step, carried):
            pieces = [
                by_col[group, pl.ds(first, blocks, stride=STEPS)].reshape(half, NDISP)
                for first in (step, STEPS - 1 - step)
            ]
            put(h_cost, (step,), ordered(jnp.concatenate(pieces, axis=0).astype(jnp.bfloat16)))
            return carried

        lax.fori_loop(0, STEPS, turn, 0, unroll=True)

        def pair(index, carried):
            start = 2 * index
            first = advance(take(h_cost, start), take(h_cost, start + 1))[0]
            second = take(h_cost, start + 1)

            def move(step, states):
                here = take(h_cost, step)
                return tuple(advance(state, here)[0] for state in states)

            states = lax.fori_loop(start + 2, STEPS, move, (first, second))
            for num, state in enumerate(states):
                lay(turned, (num,), state)
                block = upright(turned[num], 3) + PENALTY_LARGE
                for way in range(2):
                    value = block[way * half : way * half + half].reshape(blocks, *vreg)
                    landed[way, group, :, start + num] = value
            return carried

        lax.fori_loop(0, STEPS // 2, pair, 0)

    for group in range(groups):
        landings(group)

        def one_block(block, carried):
            transfer(group, block)
            return carried

        lax.fori_loop(0, blocks, one_block, 0)

    def v_turn(turn):
        lower_half = row > rows - 1 - row
        backward = lower_half != (turn == 1)
        way = backward.astype(jnp.int32)
        step = 1 - 2 * way
        has_source = (row - step >= 0) & (row - step < rows)
        has_target = (row + step >= 0) & (row + step < rows)
        copy = pltpu.make_async_remote_copy(
            src_ref=v_send.at[way],
            dst_ref=v_recv.at[way],
            send_sem=v_send_sem.at[way],
            recv_sem=v_recv_sem.at[way],
            device_id={"row": row + step},
            device_id_type=MESH,
        )
        return copy, has_source, has_target, way, backward

    def column_sweep(turn):
        copy, has_source, has_target, way, backward = v_turn(turn)

        @pl.when(has_source)
        def _():
            copy.wait_recv()

        @pl.when(jnp.logical_not(has_source))
        def _():
            v_recv[way] = jnp.zeros(v_recv.shape[1:], jnp.float32)

        def body(index, state):
            place = jnp.where(backward, tile_rows - 1 - index, index)
            state, lowest = advance(state, take(v_cost, place))
            state = tuple(value - lowest for value in state)
            lay(v_path, (way, place), state)
            return state

        state = lax.fori_loop(0, tile_rows, body, take(v_recv, way))
        for lead in range(LEADS):
            v_send[way, lead] = state[lead]

        @pl.when(has_target)
        def _():
            copy.start()

    def vertical(point):
        outer = jnp.minimum(row, rows - 1 - row)
        for turn, stage in enumerate((outer, rows - 1 - outer)):

            @pl.when(stage * 4 // rows == point)
            def _():
                column_sweep(turn)

    def entry_copy(way, tile, y, target):
        return pltpu.make_async_remote_copy(
            src_ref=entry_out.at[way, tile],
            dst_ref=entry_in.at[way, y],
            send_sem=entry_send_sem.at[way, tile],
            recv_sem=entry_recv_sem.at[way, y],
            device_id={"col": target},
            device_id_type=MESH,
        )

    def everywhere(value):
        for shift in (4, 2, 1):
            value = jnp.minimum(value, pltpu.roll(value, shift, 0))
        return value

    def cross(way, tile, block, state):
        group, place = tile // SUBS, tile % SUBS
        lows, best = [], None
        for part in range(0, STEPS, SUBS):
            where = pl.ds(part, SUBS)
            gone = state + reach[way, group, block, where, place, :]
            low = jnp.broadcast_to(jnp.min(gone, axis=1, keepdims=True), vreg)
            landing = low + landed[way, group, block, where, place, :]
            lows.append(low)
            best = landing if best is None else jnp.minimum(best, landing)
        still = local[way, group, block, pl.ds(2 * STEPS, 1), place, :]
        best = jnp.minimum(best, state + still)
        for part in range(0, 2 * STEPS, SUBS):
            moved = state + local[way, group, block, pl.ds(part, SUBS), place, :]
            off = part - STEPS + (part >= STEPS)
            moved = pltpu.roll(moved, off % NDISP, 1, stride=1, stride_axis=0)
            best = jnp.minimum(best, moved)
        return everywhere(best) - everywhere(lows[0])

    def tile_lines():
        for y in range(tile_rows):

            @pl.when(col != y * share)
            def _():
                volume_copy(y, y, col).wait_recv()

        def tile_line(y, carried):
            block = volume[y]
            put(v_cost, (y,), ordered(block))
            wide[y] = block.astype(jnp.float32)
            return carried

        lax.fori_loop(0, tile_rows, tile_line, 0, unroll=True)

    def tile_turns():
        def tile_turn(step, carried):
            pieces = [
                wide[y, pl.ds(first, blocks, stride=STEPS), :]
                for first in (step, STEPS - 1 - step)
                for y in range(tile_rows)
            ]
            put(t_cost, (step,), ordered(jnp.concatenate(pieces, axis=0).astype(jnp.bfloat16)))
            return carried

        lax.fori_loop(0, STEPS, tile_turn, 0, unroll=True)

    states = (jnp.zeros(vreg, jnp.float32),) * 2
    point = 0
    for number in range(cols):
        tiles = (number, cols - 1 - number)

        def one_block(index, states):
            after = []
            for way in range(2):
                block = blocks - 1 - index if way else index
                entry_out[way, tiles[way], pl.ds(block, 1), :] = states[way][0:1]
                after.append(cross(way, tiles[way], block, states[way]))
            return tuple(after)

        states = lax.fori_loop(0, blocks, one_block, states)
        for way in range(2):
            tile = tiles[way]

            @pl.when(leads & (col != tile))
            def _():
                entry_copy(way, tile, line, tile).start()

            @pl.when(leads & (col == tile))
            def _():
                entry_in[way, line] = entry_out[way, tile]

        if number == cols // 4 - 1:
            tile_lines()
        while point < 4 and number == (point + 1) * cols // 4 - 1:
            vertical(point)
            point += 1

    tile_turns()
    for y in range(tile_rows):
        total[y] = upright(v_path[0, y] + v_path[1, y], 2)

    for y in range(tile_rows):
        for way in range(2):

            @pl.when(col != y * share)
            def _():
                entry_copy(way, y, y, col).wait_recv()

    block = entry_in[...].reshape(NDISP, NDISP)
    block = sum(ordered(part) for part in split(block))
    state = tuple(block[lead * SUBS : lead * SUBS + SUBS] for lead in range(LEADS))

    def dense(index, state):
        state, lowest = advance(state, take(t_cost, index))
        state = tuple(value - lowest for value in state)
        lay(h_path, (index,), state)
        return state

    lax.fori_loop(0, STEPS, dense, state, unroll=True)

    def gather_step(step, carried):
        block = upright(h_path[step], 2)
        for way in range(2):
            where = pl.ds(STEPS - 1 - step if way else step, blocks, stride=STEPS)
            for y in range(tile_rows):
                begin = way * half + y * blocks
                total[y, where, :] = total[y, where, :] + block[begin : begin + blocks]
        return carried

    lax.fori_loop(0, STEPS, gather_step, 0, unroll=True)
    for y in range(tile_rows):
        out_ref[y] = (total[y] * 0.25).astype(jnp.bfloat16)

    for tile in range(cols):

        @pl.when(leads & (col != tile))
        def _():
            volume_copy(tile, line, tile).wait_send()
            for way in range(2):
                entry_copy(way, tile, line, tile).wait_send()

    for turn in range(2):
        copy, _, has_target, _, _ = v_turn(turn)

        @pl.when(has_target)
        def _():
            copy.wait_send()

    for down, other, k in moves:

        @pl.when(sends(down, other))
        def _():
            image_copy(down, other, col, k).wait_send()


def aggregate(tile_base, tile_width, *arrays):
    tile_rows, tile_cols = arrays[0].shape
    cols = lax.axis_size("col")
    groups = cols // SUBS
    vreg = (SUBS, NDISP)
    vregs = (LEADS, *vreg)
    blocks = tile_cols // STEPS
    tile = (tile_rows, tile_cols, NDISP)
    fields = (FIELDS * tile_rows, tile_cols)
    return pl.pallas_call(
        partial(path_kernel, tile_rows, tile_cols),
        out_shape=jax.ShapeDtypeStruct(tile, jnp.bfloat16),
        in_specs=[pl.BlockSpec(memory_space=pltpu.SMEM)] * 2
        + [pl.BlockSpec(memory_space=pltpu.HBM)] * 5,
        out_specs=pl.BlockSpec(memory_space=pltpu.VMEM),
        scratch_shapes=[
            *(pltpu.VMEM(array.shape, array.dtype) for array in arrays),
            pltpu.VMEM(fields, jnp.bfloat16),
            pltpu.VMEM((3, cols, *fields), jnp.bfloat16),
            pltpu.VMEM((2, 3 * tile_rows, (cols + 1) * tile_cols), jnp.float32),
            pltpu.VMEM((groups, tile_cols, *vreg), jnp.float32),
            pltpu.VMEM((cols, tile_cols, NDISP), jnp.bfloat16),
            pltpu.VMEM(tile, jnp.bfloat16),
            pltpu.VMEM(tile, jnp.float32),
            pltpu.VMEM((tile_rows, *vregs), jnp.float32),
            pltpu.VMEM((STEPS, *vregs), jnp.float32),
            pltpu.VMEM((STEPS, *vregs), jnp.float32),
            pltpu.VMEM((2, tile_rows, NDISP, NDISP), jnp.float32),
            pltpu.VMEM((STEPS, NDISP, NDISP), jnp.float32),
            pltpu.VMEM((2, NDISP, NDISP), jnp.float32),
            pltpu.VMEM(tile, jnp.float32),
            pltpu.VMEM((2, groups, blocks, 2 * STEPS + 1, *vreg), jnp.float32),
            pltpu.VMEM((2, groups, blocks, STEPS, *vreg), jnp.float32),
            pltpu.VMEM((2, groups, blocks, STEPS, *vreg), jnp.float32),
            pltpu.VMEM((2, cols, blocks, NDISP), jnp.float32),
            pltpu.VMEM((2, tile_rows, blocks, NDISP), jnp.float32),
            pltpu.VMEM((2, *vregs), jnp.float32),
            pltpu.VMEM((2, *vregs), jnp.float32),
            pltpu.SemaphoreType.DMA((3, cols)),
            pltpu.SemaphoreType.DMA((3, cols)),
            pltpu.SemaphoreType.DMA((cols,)),
            pltpu.SemaphoreType.DMA((tile_rows,)),
            pltpu.SemaphoreType.DMA((2, cols)),
            pltpu.SemaphoreType.DMA((2, tile_rows)),
            pltpu.SemaphoreType.DMA((2,)),
            pltpu.SemaphoreType.DMA((2,)),
            pltpu.SemaphoreType.DMA((len(arrays),)),
        ],
        compiler_params=pltpu.CompilerParams(
            collective_id=0, has_side_effects=True, vmem_limit_bytes=56 << 20
        ),
        name="paths",
    )(tile_base, tile_width, *arrays)


def on_device(
    left_image, right_image, first_weight, second_weight, third_weight, tile_base, tile_width
):
    return aggregate(
        tile_base, tile_width, left_image, right_image, first_weight.T, second_weight, third_weight
    )


def solution(mesh):
    placed = (P("row", "col"), P("row", "col"), P(), P(), P(), P("row", "col"), P("row", "col"))
    return jax.shard_map(
        on_device, mesh=mesh, in_specs=placed, out_specs=P("row", "col", None), check_vma=False
    )
```

```python
from functools import partial

import jax
import jax.numpy as jnp
from jax import lax
from jax.experimental import pallas as pl
from jax.experimental.pallas import tpu as pltpu
from jax.sharding import PartitionSpec as P

NDISP = 128
MESH = pl.DeviceIdType.MESH


PENALTY_SMALL = 0.5
PENALTY_LARGE = 4.0
INVALID_COST = 2.0
BIG_VALUE = 1e30

RIM = 3
SUBS = 8
LEADS = NDISP // SUBS
STEPS = 16
FIELDS = 4
POINTS = (2, 5, 8)


def least(values):
    values = list(values)
    while len(values) > 1:
        pairs = [jnp.minimum(values[i], values[i + 1]) for i in range(0, len(values) - 1, 2)]
        values = pairs + ([values[-1]] if len(values) % 2 else [])
    return values[0]


def split(value):
    high = value.astype(jnp.bfloat16)
    rest = value - high.astype(jnp.float32)
    mid = rest.astype(jnp.bfloat16)
    low = (rest - mid.astype(jnp.float32)).astype(jnp.bfloat16)
    return high, mid, low


def owned(col, cols, tile_rows):
    return col // (cols // tile_rows)


def layer(source, weight, span, out_rows, rectify, inside):
    chans, length = source.shape
    outs = weight.shape[0]
    if chans == 1:
        stacked = jnp.concatenate(
            [pltpu.roll(source, 1, 1), source, pltpu.roll(source, length - 1, 1)], axis=0
        ).astype(jnp.bfloat16)
        result = jnp.zeros((outs, out_rows * span), jnp.float32)
        for row_off in range(3):
            result = result + jnp.dot(
                weight[:, row_off * 3 : (row_off + 1) * 3],
                stacked[:, row_off * span : (row_off + out_rows) * span],
                preferred_element_type=jnp.float32,
            )
    else:
        taps = jnp.concatenate(
            [
                jnp.concatenate(
                    [
                        weight[:, (3 * row_off + col_off) * chans :][:, :chans]
                        for row_off in range(3)
                    ],
                    axis=1,
                )
                for col_off in range(3)
            ],
            axis=0,
        )
        stacked = jnp.concatenate(
            [source[:, r * span : (r + out_rows) * span] for r in range(3)], axis=0
        )
        parts = jnp.dot(taps, stacked.astype(jnp.bfloat16), preferred_element_type=jnp.float32)
        result = (
            pltpu.roll(parts[:outs], 1, 1)
            + parts[outs : 2 * outs]
            + pltpu.roll(parts[2 * outs :], out_rows * span - 1, 1)
        )
    if rectify:
        result = jnp.maximum(result, 0.0)
    return (result * inside).astype(jnp.bfloat16).astype(jnp.float32)


def path_kernel(
    tile_rows,
    tile_cols,
    base_ref,
    width_ref,
    left_hbm,
    right_hbm,
    first_hbm,
    second_hbm,
    third_hbm,
    out_ref,
    left_ref,
    right_ref,
    first_ref,
    second_ref,
    third_ref,
    own_ref,
    gathered,
    lines,
    by_col,
    by_tile,
    volume,
    wide,
    v_cost,
    h_cost,
    t_cost,
    v_path,
    h_path,
    turned,
    total,
    local,
    reach,
    landed,
    entry_out,
    entry_in,
    v_send,
    v_recv,
    image_send_sem,
    image_recv_sem,
    volume_send_sem,
    volume_recv_sem,
    entry_send_sem,
    entry_recv_sem,
    v_send_sem,
    v_recv_sem,
    load_sem,
):
    cols, rows = lax.axis_size("col"), lax.axis_size("row")
    col, row = lax.axis_index("col"), lax.axis_index("row")
    share = cols // tile_rows
    line = owned(col, cols, tile_rows)
    leads = lax.rem(col, share) == 0
    blocks = tile_cols // STEPS
    groups = cols // SUBS
    vreg = (SUBS, NDISP)
    half = blocks * SUBS
    barrier = pltpu.get_barrier_semaphore()
    loads = [
        pltpu.make_async_copy(source, target, load_sem.at[num])
        for num, (source, target) in enumerate(
            (
                (left_hbm, left_ref),
                (right_hbm, right_ref),
                (first_hbm, first_ref),
                (second_hbm, second_ref),
                (third_hbm, third_ref),
            )
        )
    ]
    for load in loads:
        load.start()
    far = sorted(range(cols), key=lambda k: -min(k, cols - k))
    moves = [(down, lax.rem(col + k, cols), k) for down in (0, -1, 1) for k in far if k or down]

    def wanted(down, target):
        line = owned(target, cols, tile_rows)
        if down == 0:
            return jnp.bool_(True)
        return line < RIM if down > 0 else line >= tile_rows - RIM

    def sends(down, target):
        return wanted(down, target) & (row + down >= 0) & (row + down < rows)

    def receives(down):
        return wanted(down, col) & (row - down >= 0) & (row - down < rows)

    count = jnp.int32(0)
    for step in (-1, 1):
        there = (row + step >= 0) & (row + step < rows)

        @pl.when(there)
        def _():
            pl.semaphore_signal(
                barrier, inc=1, device_id={"row": row + step}, device_id_type=MESH
            )

        count = count + there.astype(jnp.int32)
    for down, other, k in moves:

        @pl.when(receives(down))
        def _():
            pl.semaphore_signal(
                barrier,
                inc=1,
                device_id={"row": row - down, "col": other},
                device_id_type=MESH,
            )

        count = count + sends(down, other).astype(jnp.int32)
    loads[0].wait()
    loads[1].wait()
    fields = [
        left_ref[...].astype(jnp.float32),
        right_ref[...].astype(jnp.float32),
        jnp.full(left_ref.shape, base_ref[0, 0].astype(jnp.float32)),
        jnp.full(left_ref.shape, width_ref[0, 0].astype(jnp.float32)),
    ]
    value = jnp.concatenate(fields, axis=0).astype(jnp.bfloat16)
    own_ref[...] = value
    for down in (-1, 1):

        @pl.when(jnp.logical_not(receives(down)))
        def _():
            gathered[1 - down] = jnp.zeros(gathered.shape[1:], jnp.bfloat16)

    gathered[1, col] = value
    pl.semaphore_wait(barrier, count)

    def image_copy(down, target, source, slot):
        return pltpu.make_async_remote_copy(
            src_ref=own_ref,
            dst_ref=gathered.at[1 - down, source],
            send_sem=image_send_sem.at[1 - down, slot],
            recv_sem=image_recv_sem.at[1 - down, source],
            device_id={"row": row + down, "col": target},
            device_id_type=MESH,
        )

    for down, other, k in moves:

        @pl.when(sends(down, other))
        def _():
            image_copy(down, other, col, k).start()

    for down, other, k in moves:

        @pl.when(receives(down))
        def _():
            image_copy(down, other, other, k).wait_recv()

    def volume_copy(tile, y, slot):
        return pltpu.make_async_remote_copy(
            src_ref=by_tile.at[tile],
            dst_ref=volume.at[y],
            send_sem=volume_send_sem.at[tile],
            recv_sem=volume_recv_sem.at[y],
            device_id={"col": slot},
            device_id_type=MESH,
        )

    for load in loads[2:]:
        load.wait()
    weights = (first_ref[...].astype(jnp.float32).T.astype(jnp.bfloat16), second_ref[...], third_ref[...])
    span = (cols + 1) * tile_cols
    column = lax.broadcasted_iota(jnp.int32, (1, span), 1)
    for down in range(3):
        for other in range(cols):
            pair = gathered[down, other, : 2 * tile_rows].astype(jnp.float32)
            for image in range(2):
                lines[
                    image,
                    down * tile_rows : (down + 1) * tile_rows,
                    other * tile_cols : (other + 1) * tile_cols,
                ] = pair[image * tile_rows : (image + 1) * tile_rows]
    lines[:, :, cols * tile_cols :] = jnp.zeros((2, 3 * tile_rows, tile_cols), jnp.float32)

    def tower(image):
        current = jnp.concatenate(
            [
                lines[image, pl.ds(tile_rows + line - RIM + i, 1), :]
                for i in range(2 * RIM + 1)
            ],
            axis=1,
        )
        for num in range(RIM):
            edge = RIM - 1 - num
            inside = []
            for i in range(-edge, edge + 1):
                place = row * tile_rows + line + i
                limit = jnp.where((place >= 0) & (place < rows * tile_rows), cols * tile_cols, 0)
                inside.append(jnp.where(column < limit, 1.0, 0.0))
            inside = jnp.concatenate(inside, axis=1)
            current = layer(current, weights[num], span, 2 * edge + 1, num < RIM - 1, inside)
        return current

    left = tower(0)
    right = tower(1)
    ext = 2 * tile_cols
    flip = lax.broadcasted_iota(jnp.int32, (ext, ext), 0) + lax.broadcasted_iota(
        jnp.int32, (ext, ext), 1
    )
    flip = (flip == ext - 1).astype(jnp.float32).astype(jnp.bfloat16)
    shifts = lax.broadcasted_iota(jnp.int32, (tile_cols, NDISP), 1).astype(jnp.float32)
    for tile in range(cols):
        begin = tile * tile_cols
        own = left[:, begin : begin + tile_cols].T
        before = (begin or span) - tile_cols
        other = jnp.concatenate(
            [right[:, before : before + tile_cols], right[:, begin : begin + tile_cols]], axis=1
        )
        other = jnp.dot(other.astype(jnp.bfloat16), flip, preferred_element_type=jnp.float32)
        own_norm = jnp.maximum(jnp.sqrt(jnp.sum(own * own, axis=1, keepdims=True)), 1.0)
        other_norm = jnp.maximum(jnp.sqrt(jnp.sum(other * other, axis=0, keepdims=True)), 1.0)
        products = jnp.dot(
            own.astype(jnp.bfloat16),
            other.astype(jnp.bfloat16),
            preferred_element_type=jnp.float32,
        )
        cosine = products * (1.0 / own_norm) * (1.0 / other_norm)
        cosine = pltpu.roll(cosine, ext - tile_cols + 1, 1, stride=1, stride_axis=0)
        extent = gathered[1, tile, 2 * tile_rows :].astype(jnp.float32)
        base, width = extent[0:1], extent[tile_rows : tile_rows + 1]
        in_range = (shifts >= base) & (shifts < base + width)
        cost = jnp.where(in_range, 1.0 - cosine[:, :NDISP], INVALID_COST).astype(jnp.bfloat16)
        by_tile[tile] = cost
        by_col[tile // SUBS, :, tile % SUBS, :] = cost.astype(jnp.float32)

    for tile in range(cols):

        @pl.when(leads & (col != tile))
        def _():
            volume_copy(tile, line, tile).start()

        @pl.when(leads & (col == tile))
        def _():
            volume[line] = by_tile[tile]

    sub = lax.broadcasted_iota(jnp.int32, vreg, 0)
    lane = lax.broadcasted_iota(jnp.int32, vreg, 1)
    first_edge = jnp.where(sub == 0, BIG_VALUE, PENALTY_SMALL)
    last_edge = jnp.where(sub == SUBS - 1, BIG_VALUE, PENALTY_SMALL)
    near_row = lax.broadcasted_iota(jnp.int32, (NDISP, NDISP), 0)
    near_col = lax.broadcasted_iota(jnp.int32, (NDISP, NDISP), 1)
    order = ((near_row % SUBS) * LEADS + near_row // SUBS == near_col).astype(jnp.float32)
    order = order.astype(jnp.bfloat16)
    same = (near_row == near_col).astype(jnp.float32).astype(jnp.bfloat16)

    def ordered(block):
        return lax.dot_general(
            order, block, (((1,), (1,)), ((), ())), preferred_element_type=jnp.float32
        )

    def upright(block, parts):
        return sum(
            lax.dot_general(
                same, part, (((1,), (1,)), ((), ())), preferred_element_type=jnp.float32
            )
            for part in split(block)[:parts]
        )

    def lay(ref, where, state):
        for lead in range(LEADS):
            ref[(*where, pl.ds(lead, SUBS, stride=LEADS), slice(None))] = state[lead]

    def put(ref, where, block):
        for lead in range(LEADS):
            ref[(*where, lead)] = block[lead * SUBS : lead * SUBS + SUBS]

    def take(ref, *where):
        return tuple(ref[(*where, lead)] for lead in range(LEADS))

    def advance(state, here):
        lowest = least(state)
        lowest = jnp.minimum(lowest, pltpu.roll(lowest, 4, 0))
        turned = [pltpu.roll(lowest, shift, 0) for shift in (1, 2, 3)]
        lowest = jnp.minimum(
            jnp.minimum(lowest, turned[0]), jnp.minimum(turned[1], turned[2])
        )
        jump = lowest + PENALTY_LARGE
        below = pltpu.roll(state[LEADS - 1], 1, 0) + first_edge
        above = pltpu.roll(state[0], SUBS - 1, 0) + last_edge
        ext = [below, *(value + PENALTY_SMALL for value in state), above]
        new = []
        for lead in range(LEADS):
            near = jnp.minimum(state[lead], jnp.minimum(ext[lead], ext[lead + 2]))
            new.append(jnp.minimum(near, jump) + here[lead])
        return tuple(new), lowest

    def slot_of(off):
        return 2 * STEPS if off == 0 else off + STEPS - (off > 0)

    def transfer(group, block):
        shifted = {}

        def cost_at(place, off):
            if (place, off) not in shifted:
                here = by_col[group, block * STEPS + place]
                if off:
                    inside = lane < NDISP - off if off > 0 else lane >= -off
                    here = jnp.where(inside, pltpu.roll(here, -off % NDISP, 1), BIG_VALUE)
                shifted[place, off] = here
            return shifted[place, off]

        for way in range(2):
            reached = {0: jnp.zeros(vreg, jnp.float32)}
            reach[way, group, block, 0] = reached[0]
            for step in range(STEPS):
                after = {}
                for off in range(-step - 1, step + 2):
                    cost = cost_at(STEPS - 1 - step if way else step, off)
                    side = [reached[o] for o in (off - 1, off + 1) if o in reached]
                    near = least(side) + PENALTY_SMALL if side else None
                    if off in reached:
                        near = reached[off] if near is None else jnp.minimum(reached[off], near)
                    after[off] = near + cost
                reached = after
                if step < STEPS - 1:
                    reach[way, group, block, step + 1] = least(reached.values())
            for off, value in reached.items():
                local[way, group, block, slot_of(off)] = value

    def landings(group):
        def turn(step, carried):
            pieces = [
                by_col[group, pl.ds(first, blocks, stride=STEPS)].reshape(half, NDISP)
                for first in (step, STEPS - 1 - step)
            ]
            put(h_cost, (step,), ordered(jnp.concatenate(pieces, axis=0).astype(jnp.bfloat16)))
            return carried

        lax.fori_loop(0, STEPS, turn, 0, unroll=True)

        def pair(index, carried):
            start = 2 * index
            first = advance(take(h_cost, start), take(h_cost, start + 1))[0]
            second = take(h_cost, start + 1)

            def move(number, states):
                for step in (0, 1):
                    here = take(h_cost, 2 * number + step)
                    states = tuple(advance(state, here)[0] for state in states)
                return states

            states = lax.fori_loop(index + 1, STEPS // 2, move, (first, second))
            for num, state in enumerate(states):
                lay(turned, (start + num,), state)
            return carried

        lax.fori_loop(0, STEPS // 2, pair, 0)
        for start in range(STEPS):
            block = upright(turned[start], 3) + PENALTY_LARGE
            for way in range(2):
                value = block[way * half : way * half + half].reshape(blocks, *vreg)
                landed[way, group, :, start] = value

    for group in range(groups):
        landings(group)

        def one_block(block, carried):
            transfer(group, block)
            return carried

        lax.fori_loop(0, blocks, one_block, 0)

    def v_turn(turn):
        lower_half = row > rows - 1 - row
        backward = lower_half != (turn == 1)
        way = backward.astype(jnp.int32)
        step = 1 - 2 * way
        has_source = (row - step >= 0) & (row - step < rows)
        has_target = (row + step >= 0) & (row + step < rows)
        copy = pltpu.make_async_remote_copy(
            src_ref=v_send.at[way],
            dst_ref=v_recv.at[way],
            send_sem=v_send_sem.at[way],
            recv_sem=v_recv_sem.at[way],
            device_id={"row": row + step},
            device_id_type=MESH,
        )
        return copy, has_source, has_target, way, backward

    def column_sweep(turn):
        copy, has_source, has_target, way, backward = v_turn(turn)

        @pl.when(has_source)
        def _():
            copy.wait_recv()

        @pl.when(jnp.logical_not(has_source))
        def _():
            v_recv[way] = jnp.zeros(v_recv.shape[1:], jnp.float32)

        def body(index, state):
            place = jnp.where(backward, tile_rows - 1 - index, index)
            state, lowest = advance(state, take(v_cost, place))
            state = tuple(value - lowest for value in state)
            lay(v_path, (way, place), state)
            return state

        state = lax.fori_loop(0, tile_rows, body, take(v_recv, way))
        for lead in range(LEADS):
            v_send[way, lead] = state[lead]

        @pl.when(has_target)
        def _():
            copy.start()

    def vertical(point):
        outer = jnp.minimum(row, rows - 1 - row)
        for turn, stage in enumerate((outer, rows - 1 - outer)):

            @pl.when(stage * 4 // rows == point)
            def _():
                column_sweep(turn)

    def entry_copy(way, tile, y, target):
        return pltpu.make_async_remote_copy(
            src_ref=entry_out.at[way, tile],
            dst_ref=entry_in.at[way, y],
            send_sem=entry_send_sem.at[way, tile],
            recv_sem=entry_recv_sem.at[way, y],
            device_id={"col": target},
            device_id_type=MESH,
        )

    def everywhere(value):
        for shift in (4, 2, 1):
            value = jnp.minimum(value, pltpu.roll(value, shift, 0))
        return value

    def cross(way, tile, block, state):
        group, place = tile // SUBS, tile % SUBS
        lows, best = [], None
        for part in range(0, STEPS, SUBS):
            where = pl.ds(part, SUBS)
            gone = state + reach[way, group, block, where, place, :]
            low = jnp.broadcast_to(jnp.min(gone, axis=1, keepdims=True), vreg)
            landing = low + landed[way, group, block, where, place, :]
            lows.append(low)
            best = landing if best is None else jnp.minimum(best, landing)
        still = local[way, group, block, pl.ds(2 * STEPS, 1), place, :]
        best = jnp.minimum(best, state + still)
        for part in range(0, 2 * STEPS, SUBS):
            moved = state + local[way, group, block, pl.ds(part, SUBS), place, :]
            off = part - STEPS + (part >= STEPS)
            moved = pltpu.roll(moved, off % NDISP, 1, stride=1, stride_axis=0)
            best = jnp.minimum(best, moved)
        return everywhere(best) - everywhere(lows[0])

    def tile_lines():
        for y in range(tile_rows):

            @pl.when(col != y * share)
            def _():
                volume_copy(y, y, col).wait_recv()

        def tile_line(y, carried):
            block = volume[y]
            put(v_cost, (y,), ordered(block))
            return carried

        lax.fori_loop(0, tile_rows, tile_line, 0, unroll=True)

    def tile_turns():
        for y in range(tile_rows):
            wide[y] = volume[y].astype(jnp.float32)
        def tile_turn(step, carried):
            pieces = [
                wide[y, pl.ds(first, blocks, stride=STEPS), :]
                for first in (step, STEPS - 1 - step)
                for y in range(tile_rows)
            ]
            put(t_cost, (step,), ordered(jnp.concatenate(pieces, axis=0).astype(jnp.bfloat16)))
            return carried

        lax.fori_loop(0, STEPS, tile_turn, 0, unroll=True)

    states = (jnp.zeros(vreg, jnp.float32),) * 2
    point = 0
    for number in range(cols):
        tiles = (number, cols - 1 - number)

        def one_block(index, states):
            after = []
            for way in range(2):
                block = blocks - 1 - index if way else index
                entry_out[way, tiles[way], pl.ds(block, 1), :] = states[way][0:1]
                after.append(cross(way, tiles[way], block, states[way]))
            return tuple(after)

        states = lax.fori_loop(0, blocks, one_block, states, unroll=cols <= SUBS)
        for way in range(2):
            tile = tiles[way]

            @pl.when(leads & (col != tile))
            def _():
                entry_copy(way, tile, line, tile).start()

            @pl.when(leads & (col == tile))
            def _():
                entry_in[way, line] = entry_out[way, tile]

        if number == cols // 4 - 1:
            tile_lines()
        while point < 3 and number == POINTS[point] * cols // 8 - 1:
            vertical(point)
            point += 1

    tile_turns()
    vertical(3)
    for y in range(tile_rows):
        total[y] = upright(v_path[0, y] + v_path[1, y], 2)

    for y in range(tile_rows):
        for way in range(2):

            @pl.when(col != y * share)
            def _():
                entry_copy(way, y, y, col).wait_recv()

    block = entry_in[...].reshape(NDISP, NDISP)
    block = sum(ordered(part) for part in split(block))
    state = tuple(block[lead * SUBS : lead * SUBS + SUBS] for lead in range(LEADS))

    def dense(index, state):
        state, lowest = advance(state, take(t_cost, index))
        state = tuple(value - lowest for value in state)
        lay(h_path, (index,), state)
        return state

    lax.fori_loop(0, STEPS, dense, state, unroll=True)

    def gather_step(step, carried):
        block = upright(h_path[step], 2)
        for way in range(2):
            where = pl.ds(STEPS - 1 - step if way else step, blocks, stride=STEPS)
            for y in range(tile_rows):
                begin = way * half + y * blocks
                total[y, where, :] = total[y, where, :] + block[begin : begin + blocks]
        return carried

    lax.fori_loop(0, STEPS, gather_step, 0, unroll=True)
    for y in range(tile_rows):
        out_ref[y] = (total[y] * 0.25).astype(jnp.bfloat16)

    for tile in range(cols):

        @pl.when(leads & (col != tile))
        def _():
            volume_copy(tile, line, tile).wait_send()
            for way in range(2):
                entry_copy(way, tile, line, tile).wait_send()

    for turn in range(2):
        copy, _, has_target, _, _ = v_turn(turn)

        @pl.when(has_target)
        def _():
            copy.wait_send()

    for down, other, k in moves:

        @pl.when(sends(down, other))
        def _():
            image_copy(down, other, col, k).wait_send()


def aggregate(tile_base, tile_width, *arrays):
    tile_rows, tile_cols = arrays[0].shape
    cols = lax.axis_size("col")
    groups = cols // SUBS
    vreg = (SUBS, NDISP)
    vregs = (LEADS, *vreg)
    blocks = tile_cols // STEPS
    tile = (tile_rows, tile_cols, NDISP)
    fields = (FIELDS * tile_rows, tile_cols)
    return pl.pallas_call(
        partial(path_kernel, tile_rows, tile_cols),
        out_shape=pltpu.VMEM(tile, jnp.bfloat16),
        in_specs=[pl.BlockSpec(memory_space=pltpu.SMEM)] * 2
        + [pl.BlockSpec(memory_space=pltpu.HBM)] * 5,
        out_specs=pl.BlockSpec(memory_space=pltpu.VMEM),
        scratch_shapes=[
            *(pltpu.VMEM(array.shape, array.dtype) for array in arrays),
            pltpu.VMEM(fields, jnp.bfloat16),
            pltpu.VMEM((3, cols, *fields), jnp.bfloat16),
            pltpu.VMEM((2, 3 * tile_rows, (cols + 1) * tile_cols), jnp.float32),
            pltpu.VMEM((groups, tile_cols, *vreg), jnp.float32),
            pltpu.VMEM((cols, tile_cols, NDISP), jnp.bfloat16),
            pltpu.VMEM(tile, jnp.bfloat16),
            pltpu.VMEM(tile, jnp.float32),
            pltpu.VMEM((tile_rows, *vregs), jnp.float32),
            pltpu.VMEM((STEPS, *vregs), jnp.float32),
            pltpu.VMEM((STEPS, *vregs), jnp.float32),
            pltpu.VMEM((2, tile_rows, NDISP, NDISP), jnp.float32),
            pltpu.VMEM((STEPS, NDISP, NDISP), jnp.float32),
            pltpu.VMEM((STEPS, NDISP, NDISP), jnp.float32),
            pltpu.VMEM(tile, jnp.float32),
            pltpu.VMEM((2, groups, blocks, 2 * STEPS + 1, *vreg), jnp.float32),
            pltpu.VMEM((2, groups, blocks, STEPS, *vreg), jnp.float32),
            pltpu.VMEM((2, groups, blocks, STEPS, *vreg), jnp.float32),
            pltpu.VMEM((2, cols, blocks, NDISP), jnp.float32),
            pltpu.VMEM((2, tile_rows, blocks, NDISP), jnp.float32),
            pltpu.VMEM((2, *vregs), jnp.float32),
            pltpu.VMEM((2, *vregs), jnp.float32),
            pltpu.SemaphoreType.DMA((3, cols)),
            pltpu.SemaphoreType.DMA((3, cols)),
            pltpu.SemaphoreType.DMA((cols,)),
            pltpu.SemaphoreType.DMA((tile_rows,)),
            pltpu.SemaphoreType.DMA((2, cols)),
            pltpu.SemaphoreType.DMA((2, tile_rows)),
            pltpu.SemaphoreType.DMA((2,)),
            pltpu.SemaphoreType.DMA((2,)),
            pltpu.SemaphoreType.DMA((len(arrays),)),
        ],
        compiler_params=pltpu.CompilerParams(
            collective_id=0, has_side_effects=True, vmem_limit_bytes=56 << 20
        ),
        name="paths",
    )(tile_base, tile_width, *arrays)


def on_device(
    left_image, right_image, first_weight, second_weight, third_weight, tile_base, tile_width
):
    return aggregate(
        tile_base, tile_width, left_image, right_image, first_weight.T, second_weight, third_weight
    )


def solution(mesh):
    placed = (P("row", "col"), P("row", "col"), P(), P(), P(), P("row", "col"), P("row", "col"))
    return jax.shard_map(
        on_device, mesh=mesh, in_specs=placed, out_specs=P("row", "col", None), check_vma=False
    )
```

```python
from functools import partial

import jax
import jax.numpy as jnp
from jax import lax
from jax.experimental import pallas as pl
from jax.experimental.pallas import tpu as pltpu
from jax.sharding import PartitionSpec as P

NDISP = 128
MESH = pl.DeviceIdType.MESH


PENALTY_SMALL = 0.5
PENALTY_LARGE = 4.0
INVALID_COST = 2.0
BIG_VALUE = 1e30

RIM = 3
SUBS = 8
LEADS = NDISP // SUBS
STEPS = 16
FIELDS = 4
POINTS = (3, 5, 8)


def least(values):
    values = list(values)
    while len(values) > 1:
        pairs = [jnp.minimum(values[i], values[i + 1]) for i in range(0, len(values) - 1, 2)]
        values = pairs + ([values[-1]] if len(values) % 2 else [])
    return values[0]


def split(value):
    high = value.astype(jnp.bfloat16)
    rest = value - high.astype(jnp.float32)
    mid = rest.astype(jnp.bfloat16)
    low = (rest - mid.astype(jnp.float32)).astype(jnp.bfloat16)
    return high, mid, low


def owned(col, cols, tile_rows):
    return col // (cols // tile_rows)


def layer(source, weight, span, out_rows, rectify, inside):
    chans, length = source.shape
    outs = weight.shape[0]
    if chans == 1:
        stacked = jnp.concatenate(
            [pltpu.roll(source, 1, 1), source, pltpu.roll(source, length - 1, 1)], axis=0
        ).astype(jnp.bfloat16)
        result = jnp.zeros((outs, out_rows * span), jnp.float32)
        for row_off in range(3):
            result = result + jnp.dot(
                weight[:, row_off * 3 : (row_off + 1) * 3],
                stacked[:, row_off * span : (row_off + out_rows) * span],
                preferred_element_type=jnp.float32,
            )
    else:
        taps = jnp.concatenate(
            [
                jnp.concatenate(
                    [
                        weight[:, (3 * row_off + col_off) * chans :][:, :chans]
                        for row_off in range(3)
                    ],
                    axis=1,
                )
                for col_off in range(3)
            ],
            axis=0,
        )
        stacked = jnp.concatenate(
            [source[:, r * span : (r + out_rows) * span] for r in range(3)], axis=0
        )
        parts = jnp.dot(taps, stacked.astype(jnp.bfloat16), preferred_element_type=jnp.float32)
        result = (
            pltpu.roll(parts[:outs], 1, 1)
            + parts[outs : 2 * outs]
            + pltpu.roll(parts[2 * outs :], out_rows * span - 1, 1)
        )
    if rectify:
        result = jnp.maximum(result, 0.0)
    return (result * inside).astype(jnp.bfloat16).astype(jnp.float32)


def path_kernel(
    tile_rows,
    tile_cols,
    base_ref,
    width_ref,
    left_hbm,
    right_hbm,
    first_hbm,
    second_hbm,
    third_hbm,
    out_ref,
    left_ref,
    right_ref,
    first_ref,
    second_ref,
    third_ref,
    own_ref,
    gathered,
    lines,
    by_col,
    by_tile,
    volume,
    wide,
    v_cost,
    h_cost,
    t_cost,
    v_path,
    h_path,
    turned,
    total,
    outside,
    local,
    reach,
    landed,
    entry_out,
    entry_in,
    v_send,
    v_recv,
    image_send_sem,
    image_recv_sem,
    volume_send_sem,
    volume_recv_sem,
    entry_send_sem,
    entry_recv_sem,
    v_send_sem,
    v_recv_sem,
    load_sem,
):
    cols, rows = lax.axis_size("col"), lax.axis_size("row")
    col, row = lax.axis_index("col"), lax.axis_index("row")
    share = cols // tile_rows
    line = owned(col, cols, tile_rows)
    leads = lax.rem(col, share) == 0
    blocks = tile_cols // STEPS
    groups = cols // SUBS
    vreg = (SUBS, NDISP)
    half = blocks * SUBS
    barrier = pltpu.get_barrier_semaphore()
    loads = [
        pltpu.make_async_copy(source, target, load_sem.at[num])
        for num, (source, target) in enumerate(
            (
                (left_hbm, left_ref),
                (right_hbm, right_ref),
                (first_hbm, first_ref),
                (second_hbm, second_ref),
                (third_hbm, third_ref),
            )
        )
    ]
    for load in loads:
        load.start()
    far = sorted(range(cols), key=lambda k: -min(k, cols - k))
    moves = [(down, lax.rem(col + k, cols), k) for down in (0, -1, 1) for k in far if k or down]

    def wanted(down, target):
        line = owned(target, cols, tile_rows)
        if down == 0:
            return jnp.bool_(True)
        return line < RIM if down > 0 else line >= tile_rows - RIM

    def sends(down, target):
        return wanted(down, target) & (row + down >= 0) & (row + down < rows)

    def receives(down):
        return wanted(down, col) & (row - down >= 0) & (row - down < rows)

    count = jnp.int32(0)
    for step in (-1, 1):
        there = (row + step >= 0) & (row + step < rows)

        @pl.when(there)
        def _():
            pl.semaphore_signal(
                barrier, inc=1, device_id={"row": row + step}, device_id_type=MESH
            )

        count = count + there.astype(jnp.int32)
    for down, other, k in moves:

        @pl.when(receives(down))
        def _():
            pl.semaphore_signal(
                barrier,
                inc=1,
                device_id={"row": row - down, "col": other},
                device_id_type=MESH,
            )

        count = count + sends(down, other).astype(jnp.int32)
    loads[0].wait()
    loads[1].wait()
    fields = [
        left_ref[...].astype(jnp.float32),
        right_ref[...].astype(jnp.float32),
        jnp.full(left_ref.shape, base_ref[0, 0].astype(jnp.float32)),
        jnp.full(left_ref.shape, width_ref[0, 0].astype(jnp.float32)),
    ]
    value = jnp.concatenate(fields, axis=0).astype(jnp.bfloat16)
    own_ref[...] = value
    for down in (-1, 1):

        @pl.when(jnp.logical_not(receives(down)))
        def _():
            gathered[1 - down] = jnp.zeros(gathered.shape[1:], jnp.bfloat16)

    gathered[1, col] = value
    pl.semaphore_wait(barrier, count)

    def image_copy(down, target, source, slot):
        return pltpu.make_async_remote_copy(
            src_ref=own_ref,
            dst_ref=gathered.at[1 - down, source],
            send_sem=image_send_sem.at[1 - down, slot],
            recv_sem=image_recv_sem.at[1 - down, source],
            device_id={"row": row + down, "col": target},
            device_id_type=MESH,
        )

    for down, other, k in moves:

        @pl.when(sends(down, other))
        def _():
            image_copy(down, other, col, k).start()

    for down, other, k in moves:

        @pl.when(receives(down))
        def _():
            image_copy(down, other, other, k).wait_recv()

    def volume_copy(tile, y, slot):
        return pltpu.make_async_remote_copy(
            src_ref=by_tile.at[tile],
            dst_ref=volume.at[y],
            send_sem=volume_send_sem.at[tile],
            recv_sem=volume_recv_sem.at[y],
            device_id={"col": slot},
            device_id_type=MESH,
        )

    for load in loads[2:]:
        load.wait()
    weights = (first_ref[...].astype(jnp.float32).T.astype(jnp.bfloat16), second_ref[...], third_ref[...])
    span = (cols + 1) * tile_cols
    column = lax.broadcasted_iota(jnp.int32, (1, span), 1)
    for down in range(3):
        for other in range(cols):
            pair = gathered[down, other, : 2 * tile_rows].astype(jnp.float32)
            for image in range(2):
                lines[
                    image,
                    down * tile_rows : (down + 1) * tile_rows,
                    other * tile_cols : (other + 1) * tile_cols,
                ] = pair[image * tile_rows : (image + 1) * tile_rows]
    lines[:, :, cols * tile_cols :] = jnp.zeros((2, 3 * tile_rows, tile_cols), jnp.float32)

    def tower(image):
        current = jnp.concatenate(
            [
                lines[image, pl.ds(tile_rows + line - RIM + i, 1), :]
                for i in range(2 * RIM + 1)
            ],
            axis=1,
        )
        for num in range(RIM):
            edge = RIM - 1 - num
            inside = []
            for i in range(-edge, edge + 1):
                place = row * tile_rows + line + i
                limit = jnp.where((place >= 0) & (place < rows * tile_rows), cols * tile_cols, 0)
                inside.append(jnp.where(column < limit, 1.0, 0.0))
            inside = jnp.concatenate(inside, axis=1)
            current = layer(current, weights[num], span, 2 * edge + 1, num < RIM - 1, inside)
        return current

    left = tower(0)
    right = tower(1)
    ext = 2 * tile_cols
    flip = lax.broadcasted_iota(jnp.int32, (ext, ext), 0) + lax.broadcasted_iota(
        jnp.int32, (ext, ext), 1
    )
    flip = (flip == ext - 1).astype(jnp.float32).astype(jnp.bfloat16)
    shifts = lax.broadcasted_iota(jnp.int32, (tile_cols, NDISP), 1).astype(jnp.float32)
    for tile in range(cols):
        begin = tile * tile_cols
        own = left[:, begin : begin + tile_cols].T
        before = (begin or span) - tile_cols
        other = jnp.concatenate(
            [right[:, before : before + tile_cols], right[:, begin : begin + tile_cols]], axis=1
        )
        other = jnp.dot(other.astype(jnp.bfloat16), flip, preferred_element_type=jnp.float32)
        own_norm = jnp.maximum(jnp.sqrt(jnp.sum(own * own, axis=1, keepdims=True)), 1.0)
        other_norm = jnp.maximum(jnp.sqrt(jnp.sum(other * other, axis=0, keepdims=True)), 1.0)
        products = jnp.dot(
            own.astype(jnp.bfloat16),
            other.astype(jnp.bfloat16),
            preferred_element_type=jnp.float32,
        )
        cosine = products * (1.0 / own_norm) * (1.0 / other_norm)
        cosine = pltpu.roll(cosine, ext - tile_cols + 1, 1, stride=1, stride_axis=0)
        extent = gathered[1, tile, 2 * tile_rows :].astype(jnp.float32)
        base, width = extent[0:1], extent[tile_rows : tile_rows + 1]
        in_range = (shifts >= base) & (shifts < base + width)
        cost = jnp.where(in_range, 1.0 - cosine[:, :NDISP], INVALID_COST).astype(jnp.bfloat16)
        by_tile[tile] = cost
        cost = cost.astype(jnp.float32)
        for block in range(blocks):
            by_col[tile, :, block, :] = cost[block * STEPS : (block + 1) * STEPS]

    for tile in range(cols):

        @pl.when(leads & (col != tile))
        def _():
            volume_copy(tile, line, tile).start()

        @pl.when(leads & (col == tile))
        def _():
            volume[line] = by_tile[tile]

    sub = lax.broadcasted_iota(jnp.int32, vreg, 0)
    lane = lax.broadcasted_iota(jnp.int32, vreg, 1)
    first_edge = jnp.where(sub == 0, BIG_VALUE, PENALTY_SMALL)
    last_edge = jnp.where(sub == SUBS - 1, BIG_VALUE, PENALTY_SMALL)
    near_row = lax.broadcasted_iota(jnp.int32, (NDISP, NDISP), 0)
    near_col = lax.broadcasted_iota(jnp.int32, (NDISP, NDISP), 1)
    order = ((near_row % SUBS) * LEADS + near_row // SUBS == near_col).astype(jnp.float32)
    order = order.astype(jnp.bfloat16)
    same = (near_row == near_col).astype(jnp.float32).astype(jnp.bfloat16)

    def ordered(block):
        return lax.dot_general(
            order, block, (((1,), (1,)), ((), ())), preferred_element_type=jnp.float32
        )

    def upright(block, parts):
        return sum(
            lax.dot_general(
                same, part, (((1,), (1,)), ((), ())), preferred_element_type=jnp.float32
            )
            for part in split(block)[:parts]
        )

    def lay(ref, where, state):
        for lead in range(LEADS):
            ref[(*where, pl.ds(lead, SUBS, stride=LEADS), slice(None))] = state[lead]

    def put(ref, where, block):
        for lead in range(LEADS):
            ref[(*where, lead)] = block[lead * SUBS : lead * SUBS + SUBS]

    def take(ref, *where):
        return tuple(ref[(*where, lead)] for lead in range(LEADS))

    def advance(state, here):
        lowest = least(state)
        lowest = jnp.minimum(lowest, pltpu.roll(lowest, 4, 0))
        turned = [pltpu.roll(lowest, shift, 0) for shift in (1, 2, 3)]
        lowest = jnp.minimum(
            jnp.minimum(lowest, turned[0]), jnp.minimum(turned[1], turned[2])
        )
        jump = lowest + PENALTY_LARGE
        below = pltpu.roll(state[LEADS - 1], 1, 0) + first_edge
        above = pltpu.roll(state[0], SUBS - 1, 0) + last_edge
        ext = [below, *(value + PENALTY_SMALL for value in state), above]
        new = []
        for lead in range(LEADS):
            near = jnp.minimum(state[lead], jnp.minimum(ext[lead], ext[lead + 2]))
            new.append(jnp.minimum(near, jump) + here[lead])
        return tuple(new), lowest

    def slot_of(off):
        return 2 * STEPS if off == 0 else off + STEPS - (off > 0)

    for off in range(-STEPS, STEPS + 1):
        inside = (lane + off >= 0) & (lane + off < NDISP)
        outside[slot_of(off)] = jnp.where(inside, 0.0, BIG_VALUE)

    def transfer(way, tile):
        reached = {0: jnp.zeros(vreg, jnp.float32)}
        reach[way, tile, 0] = reached[0]
        for step in range(STEPS):
            here = by_col[tile, STEPS - 1 - step if way else step]
            after = {}
            for off in range(-step - 1, step + 2):
                cost = here
                if off:
                    cost = pltpu.roll(here, -off % NDISP, 1) + outside[slot_of(off)]
                side = [reached[o] for o in (off - 1, off + 1) if o in reached]
                near = least(side) + PENALTY_SMALL if side else None
                if off in reached:
                    near = reached[off] if near is None else jnp.minimum(reached[off], near)
                after[off] = near + cost
            reached = after
            if step < STEPS - 1:
                reach[way, tile, step + 1] = least(reached.values())
            else:
                for off, value in reached.items():
                    local[way, tile, slot_of(off)] = value
            yield

    def landings(group, works):
        def turn(step, carried):
            pieces = [
                by_col[group * SUBS : (group + 1) * SUBS, first].reshape(half, NDISP)
                for first in (step, STEPS - 1 - step)
            ]
            put(h_cost, (step,), ordered(jnp.concatenate(pieces, axis=0).astype(jnp.bfloat16)))
            return carried

        lax.fori_loop(0, STEPS, turn, 0, unroll=True)

        def pair(index, carried):
            start = 2 * index
            first = advance(take(h_cost, start), take(h_cost, start + 1))[0]
            second = take(h_cost, start + 1)

            def move(number, states):
                for step in (0, 1):
                    here = take(h_cost, 2 * number + step)
                    states = tuple(advance(state, here)[0] for state in states)
                return states

            states = lax.fori_loop(index + 1, STEPS // 2, move, (first, second))
            for num, state in enumerate(states):
                lay(turned, (start + num,), state)
            return carried

        lax.fori_loop(0, STEPS // 2, pair, 0)
        for start in range(STEPS):
            block = upright(turned[start], 3) + PENALTY_LARGE
            for way in range(2):
                value = block[way * half : way * half + half].reshape(SUBS, *vreg)
                landed[way, group * SUBS : (group + 1) * SUBS, start] = value
            for work in works:
                next(work)

    together = cols <= SUBS
    works = [transfer(0, 0), transfer(1, cols - 1)] if together else []
    for group in range(groups):
        landings(group, works)

    if not together:

        def one_tile(tile, carried):
            for way in range(2):
                for _ in transfer(way, tile):
                    pass
            return carried

        lax.fori_loop(0, cols, one_tile, 0)

    def v_turn(turn):
        lower_half = row > rows - 1 - row
        backward = lower_half != (turn == 1)
        way = backward.astype(jnp.int32)
        step = 1 - 2 * way
        has_source = (row - step >= 0) & (row - step < rows)
        has_target = (row + step >= 0) & (row + step < rows)
        copy = pltpu.make_async_remote_copy(
            src_ref=v_send.at[way],
            dst_ref=v_recv.at[way],
            send_sem=v_send_sem.at[way],
            recv_sem=v_recv_sem.at[way],
            device_id={"row": row + step},
            device_id_type=MESH,
        )
        return copy, has_source, has_target, way, backward

    def column_sweep(turn):
        copy, has_source, has_target, way, backward = v_turn(turn)

        @pl.when(has_source)
        def _():
            copy.wait_recv()

        @pl.when(jnp.logical_not(has_source))
        def _():
            v_recv[way] = jnp.zeros(v_recv.shape[1:], jnp.float32)

        def body(index, state):
            place = jnp.where(backward, tile_rows - 1 - index, index)
            state, lowest = advance(state, take(v_cost, place))
            state = tuple(value - lowest for value in state)
            lay(v_path, (way, place), state)
            return state

        state = lax.fori_loop(0, tile_rows, body, take(v_recv, way))
        for lead in range(LEADS):
            v_send[way, lead] = state[lead]

        @pl.when(has_target)
        def _():
            copy.start()

    def vertical(point):
        outer = jnp.minimum(row, rows - 1 - row)
        for turn, stage in enumerate((outer, rows - 1 - outer)):

            @pl.when(stage * 4 // rows == point)
            def _():
                column_sweep(turn)

    def entry_copy(way, tile, y, target):
        return pltpu.make_async_remote_copy(
            src_ref=entry_out.at[way, tile],
            dst_ref=entry_in.at[way, y],
            send_sem=entry_send_sem.at[way, tile],
            recv_sem=entry_recv_sem.at[way, y],
            device_id={"col": target},
            device_id_type=MESH,
        )

    def everywhere(value):
        for shift in (4, 2, 1):
            value = jnp.minimum(value, pltpu.roll(value, shift, 0))
        return value

    def cross(way, tile, block, state):
        lows, best = [], None
        for part in range(0, STEPS, SUBS):
            where = pl.ds(part, SUBS)
            gone = state + reach[way, tile, where, block, :]
            low = jnp.broadcast_to(jnp.min(gone, axis=1, keepdims=True), vreg)
            landing = low + landed[way, tile, where, block, :]
            lows.append(low)
            best = landing if best is None else jnp.minimum(best, landing)
        still = local[way, tile, pl.ds(2 * STEPS, 1), block, :]
        best = jnp.minimum(best, state + still)
        for part in range(0, 2 * STEPS, SUBS):
            moved = state + local[way, tile, pl.ds(part, SUBS), block, :]
            off = part - STEPS + (part >= STEPS)
            moved = pltpu.roll(moved, off % NDISP, 1, stride=1, stride_axis=0)
            best = jnp.minimum(best, moved)
        return everywhere(best) - everywhere(lows[0])

    def tile_wait():
        for y in range(tile_rows):

            @pl.when(col != y * share)
            def _():
                volume_copy(y, y, col).wait_recv()

    def tile_line(y):
        put(v_cost, (y,), ordered(volume[y]))

    def tile_turns():
        for y in range(tile_rows):
            wide[y] = volume[y].astype(jnp.float32)
        def tile_turn(step, carried):
            pieces = [
                wide[y, pl.ds(first, blocks, stride=STEPS), :]
                for first in (step, STEPS - 1 - step)
                for y in range(tile_rows)
            ]
            put(t_cost, (step,), ordered(jnp.concatenate(pieces, axis=0).astype(jnp.bfloat16)))
            return carried

        lax.fori_loop(0, STEPS, tile_turn, 0, unroll=True)

    states = (jnp.zeros(vreg, jnp.float32),) * 2
    point = 0
    for number in range(cols):
        tiles = (number, cols - 1 - number)

        def one_block(index, states):
            after = []
            for way in range(2):
                block = blocks - 1 - index if way else index
                entry_out[way, tiles[way], pl.ds(block, 1), :] = states[way][0:1]
                after.append(cross(way, tiles[way], block, states[way]))
            return tuple(after)

        if together:
            ahead = []
            if number < cols - 1:
                ahead = [transfer(0, number + 1), transfer(1, cols - 2 - number)]
            for index in range(blocks):
                states = one_block(index, states)
                for _ in range(len(ahead) * STEPS // blocks):
                    next(ahead[index * 2 // blocks])
                if number == cols // 4:
                    tile_line(index)
        else:
            states = lax.fori_loop(0, blocks, one_block, states)
        for way in range(2):
            tile = tiles[way]

            @pl.when(leads & (col != tile))
            def _():
                entry_copy(way, tile, line, tile).start()

            @pl.when(leads & (col == tile))
            def _():
                entry_in[way, line] = entry_out[way, tile]

        if number == cols // 4 - 1:
            tile_wait()
        if number == cols // 4 and not together:
            for y in range(tile_rows):
                tile_line(y)
        while point < 3 and number == POINTS[point] * cols // 8 - 1:
            vertical(point)
            point += 1

    tile_turns()
    vertical(3)
    for y in range(tile_rows):
        total[y] = upright(v_path[0, y] + v_path[1, y], 2)

    for y in range(tile_rows):
        for way in range(2):

            @pl.when(col != y * share)
            def _():
                entry_copy(way, y, y, col).wait_recv()

    block = entry_in[...].reshape(NDISP, NDISP)
    block = sum(ordered(part) for part in split(block))
    state = tuple(block[lead * SUBS : lead * SUBS + SUBS] for lead in range(LEADS))

    def dense(index, state):
        state, lowest = advance(state, take(t_cost, index))
        state = tuple(value - lowest for value in state)
        lay(h_path, (index,), state)
        return state

    lax.fori_loop(0, STEPS, dense, state, unroll=True)

    def gather_step(step, carried):
        block = upright(h_path[step], 2)
        for way in range(2):
            where = pl.ds(STEPS - 1 - step if way else step, blocks, stride=STEPS)
            for y in range(tile_rows):
                begin = way * half + y * blocks
                total[y, where, :] = total[y, where, :] + block[begin : begin + blocks]
        return carried

    lax.fori_loop(0, STEPS, gather_step, 0, unroll=True)
    for y in range(tile_rows):
        out_ref[y] = (total[y] * 0.25).astype(jnp.bfloat16)

    for tile in range(cols):

        @pl.when(leads & (col != tile))
        def _():
            volume_copy(tile, line, tile).wait_send()
            for way in range(2):
                entry_copy(way, tile, line, tile).wait_send()

    for turn in range(2):
        copy, _, has_target, _, _ = v_turn(turn)

        @pl.when(has_target)
        def _():
            copy.wait_send()

    for down, other, k in moves:

        @pl.when(sends(down, other))
        def _():
            image_copy(down, other, col, k).wait_send()


def aggregate(tile_base, tile_width, *arrays):
    tile_rows, tile_cols = arrays[0].shape
    cols = lax.axis_size("col")
    vreg = (SUBS, NDISP)
    vregs = (LEADS, *vreg)
    blocks = tile_cols // STEPS
    tile = (tile_rows, tile_cols, NDISP)
    fields = (FIELDS * tile_rows, tile_cols)
    return pl.pallas_call(
        partial(path_kernel, tile_rows, tile_cols),
        out_shape=pltpu.VMEM(tile, jnp.bfloat16),
        in_specs=[pl.BlockSpec(memory_space=pltpu.SMEM)] * 2
        + [pl.BlockSpec(memory_space=pltpu.HBM)] * 5,
        out_specs=pl.BlockSpec(memory_space=pltpu.VMEM),
        scratch_shapes=[
            *(pltpu.VMEM(array.shape, array.dtype) for array in arrays),
            pltpu.VMEM(fields, jnp.bfloat16),
            pltpu.VMEM((3, cols, *fields), jnp.bfloat16),
            pltpu.VMEM((2, 3 * tile_rows, (cols + 1) * tile_cols), jnp.float32),
            pltpu.VMEM((cols, STEPS, blocks, NDISP), jnp.float32),
            pltpu.VMEM((cols, tile_cols, NDISP), jnp.bfloat16),
            pltpu.VMEM(tile, jnp.bfloat16),
            pltpu.VMEM(tile, jnp.float32),
            pltpu.VMEM((tile_rows, *vregs), jnp.float32),
            pltpu.VMEM((STEPS, *vregs), jnp.float32),
            pltpu.VMEM((STEPS, *vregs), jnp.float32),
            pltpu.VMEM((2, tile_rows, NDISP, NDISP), jnp.float32),
            pltpu.VMEM((STEPS, NDISP, NDISP), jnp.float32),
            pltpu.VMEM((STEPS, NDISP, NDISP), jnp.float32),
            pltpu.VMEM(tile, jnp.float32),
            pltpu.VMEM((2 * STEPS + 1, *vreg), jnp.float32),
            pltpu.VMEM((2, cols, 2 * STEPS + 1, *vreg), jnp.float32),
            pltpu.VMEM((2, cols, STEPS, *vreg), jnp.float32),
            pltpu.VMEM((2, cols, STEPS, *vreg), jnp.float32),
            pltpu.VMEM((2, cols, blocks, NDISP), jnp.float32),
            pltpu.VMEM((2, tile_rows, blocks, NDISP), jnp.float32),
            pltpu.VMEM((2, *vregs), jnp.float32),
            pltpu.VMEM((2, *vregs), jnp.float32),
            pltpu.SemaphoreType.DMA((3, cols)),
            pltpu.SemaphoreType.DMA((3, cols)),
            pltpu.SemaphoreType.DMA((cols,)),
            pltpu.SemaphoreType.DMA((tile_rows,)),
            pltpu.SemaphoreType.DMA((2, cols)),
            pltpu.SemaphoreType.DMA((2, tile_rows)),
            pltpu.SemaphoreType.DMA((2,)),
            pltpu.SemaphoreType.DMA((2,)),
            pltpu.SemaphoreType.DMA((len(arrays),)),
        ],
        compiler_params=pltpu.CompilerParams(
            collective_id=0, has_side_effects=True, vmem_limit_bytes=56 << 20
        ),
        name="paths",
    )(tile_base, tile_width, *arrays)


def on_device(
    left_image, right_image, first_weight, second_weight, third_weight, tile_base, tile_width
):
    return aggregate(
        tile_base, tile_width, left_image, right_image, first_weight.T, second_weight, third_weight
    )


def solution(mesh):
    placed = (P("row", "col"), P("row", "col"), P(), P(), P(), P("row", "col"), P("row", "col"))
    return jax.shard_map(
        on_device, mesh=mesh, in_specs=placed, out_specs=P("row", "col", None), check_vma=False
    )
```

```python
from functools import partial

import jax
import jax.numpy as jnp
from jax import lax
from jax.experimental import pallas as pl
from jax.experimental.pallas import tpu as pltpu
from jax.sharding import PartitionSpec as P

NDISP = 128
MESH = pl.DeviceIdType.MESH


PENALTY_SMALL = 0.5
PENALTY_LARGE = 4.0
INVALID_COST = 2.0
BIG_VALUE = 1e30

RIM = 3
SUBS = 8
LEADS = NDISP // SUBS
STEPS = 16
FIELDS = 4
POINTS = (4, 6, 8)


def least(values):
    values = list(values)
    while len(values) > 1:
        pairs = [jnp.minimum(values[i], values[i + 1]) for i in range(0, len(values) - 1, 2)]
        values = pairs + ([values[-1]] if len(values) % 2 else [])
    return values[0]


def split(value):
    high = value.astype(jnp.bfloat16)
    rest = value - high.astype(jnp.float32)
    mid = rest.astype(jnp.bfloat16)
    low = (rest - mid.astype(jnp.float32)).astype(jnp.bfloat16)
    return high, mid, low


def owned(col, cols, tile_rows):
    return col // (cols // tile_rows)


def layer(source, weight, span, out_rows, rectify, inside):
    chans, length = source.shape
    outs = weight.shape[0]
    if chans == 1:
        stacked = jnp.concatenate(
            [pltpu.roll(source, 1, 1), source, pltpu.roll(source, length - 1, 1)], axis=0
        ).astype(jnp.bfloat16)
        result = jnp.zeros((outs, out_rows * span), jnp.float32)
        for row_off in range(3):
            result = result + jnp.dot(
                weight[:, row_off * 3 : (row_off + 1) * 3],
                stacked[:, row_off * span : (row_off + out_rows) * span],
                preferred_element_type=jnp.float32,
            )
    else:
        taps = jnp.concatenate(
            [
                jnp.concatenate(
                    [
                        weight[:, (3 * row_off + col_off) * chans :][:, :chans]
                        for row_off in range(3)
                    ],
                    axis=1,
                )
                for col_off in range(3)
            ],
            axis=0,
        )
        stacked = jnp.concatenate(
            [source[:, r * span : (r + out_rows) * span] for r in range(3)], axis=0
        )
        parts = jnp.dot(taps, stacked.astype(jnp.bfloat16), preferred_element_type=jnp.float32)
        result = (
            pltpu.roll(parts[:outs], 1, 1)
            + parts[outs : 2 * outs]
            + pltpu.roll(parts[2 * outs :], out_rows * span - 1, 1)
        )
    if rectify:
        result = jnp.maximum(result, 0.0)
    return (result * inside).astype(jnp.bfloat16).astype(jnp.float32)


def path_kernel(
    tile_rows,
    tile_cols,
    base_ref,
    width_ref,
    left_hbm,
    right_hbm,
    first_hbm,
    second_hbm,
    third_hbm,
    out_ref,
    left_ref,
    right_ref,
    first_ref,
    second_ref,
    third_ref,
    own_ref,
    gathered,
    lines,
    by_col,
    by_tile,
    volume,
    wide,
    v_cost,
    h_cost,
    t_cost,
    v_path,
    h_path,
    turned,
    total,
    outside,
    local,
    reach,
    landed,
    entry_out,
    entry_in,
    v_send,
    v_recv,
    image_send_sem,
    image_recv_sem,
    volume_send_sem,
    volume_recv_sem,
    entry_send_sem,
    entry_recv_sem,
    v_send_sem,
    v_recv_sem,
    load_sem,
):
    cols, rows = lax.axis_size("col"), lax.axis_size("row")
    col, row = lax.axis_index("col"), lax.axis_index("row")
    share = cols // tile_rows
    line = owned(col, cols, tile_rows)
    leads = lax.rem(col, share) == 0
    blocks = tile_cols // STEPS
    groups = cols // SUBS
    vreg = (SUBS, NDISP)
    half = blocks * SUBS
    barrier = pltpu.get_barrier_semaphore()
    loads = [
        pltpu.make_async_copy(source, target, load_sem.at[num])
        for num, (source, target) in enumerate(
            (
                (left_hbm, left_ref),
                (right_hbm, right_ref),
                (first_hbm, first_ref),
                (second_hbm, second_ref),
                (third_hbm, third_ref),
            )
        )
    ]
    for load in loads:
        load.start()
    far = sorted(range(cols), key=lambda k: -min(k, cols - k))
    moves = [(down, lax.rem(col + k, cols), k) for down in (0, -1, 1) for k in far if k or down]

    def wanted(down, target):
        line = owned(target, cols, tile_rows)
        if down == 0:
            return jnp.bool_(True)
        return line < RIM if down > 0 else line >= tile_rows - RIM

    def sends(down, target):
        return wanted(down, target) & (row + down >= 0) & (row + down < rows)

    def receives(down):
        return wanted(down, col) & (row - down >= 0) & (row - down < rows)

    count = jnp.int32(0)
    for step in (-1, 1):
        there = (row + step >= 0) & (row + step < rows)

        @pl.when(there)
        def _():
            pl.semaphore_signal(
                barrier, inc=1, device_id={"row": row + step}, device_id_type=MESH
            )

        count = count + there.astype(jnp.int32)
    for down, other, k in moves:

        @pl.when(receives(down))
        def _():
            pl.semaphore_signal(
                barrier,
                inc=1,
                device_id={"row": row - down, "col": other},
                device_id_type=MESH,
            )

        count = count + sends(down, other).astype(jnp.int32)
    loads[0].wait()
    loads[1].wait()
    fields = [
        left_ref[...].astype(jnp.float32),
        right_ref[...].astype(jnp.float32),
        jnp.full(left_ref.shape, base_ref[0, 0].astype(jnp.float32)),
        jnp.full(left_ref.shape, width_ref[0, 0].astype(jnp.float32)),
    ]
    value = jnp.concatenate(fields, axis=0).astype(jnp.bfloat16)
    own_ref[...] = value
    for down in (-1, 1):

        @pl.when(jnp.logical_not(receives(down)))
        def _():
            gathered[1 - down] = jnp.zeros(gathered.shape[1:], jnp.bfloat16)

    gathered[1, col] = value
    pl.semaphore_wait(barrier, count)

    def image_copy(down, target, source, slot):
        return pltpu.make_async_remote_copy(
            src_ref=own_ref,
            dst_ref=gathered.at[1 - down, source],
            send_sem=image_send_sem.at[1 - down, slot],
            recv_sem=image_recv_sem.at[1 - down, source],
            device_id={"row": row + down, "col": target},
            device_id_type=MESH,
        )

    for down, other, k in moves:

        @pl.when(sends(down, other))
        def _():
            image_copy(down, other, col, k).start()

    for down, other, k in moves:

        @pl.when(receives(down))
        def _():
            image_copy(down, other, other, k).wait_recv()

    def volume_copy(tile, y, slot):
        return pltpu.make_async_remote_copy(
            src_ref=by_tile.at[tile],
            dst_ref=volume.at[y],
            send_sem=volume_send_sem.at[tile],
            recv_sem=volume_recv_sem.at[y],
            device_id={"col": slot},
            device_id_type=MESH,
        )

    for load in loads[2:]:
        load.wait()
    weights = (first_ref[...].astype(jnp.float32).T.astype(jnp.bfloat16), second_ref[...], third_ref[...])
    span = (cols + 1) * tile_cols
    column = lax.broadcasted_iota(jnp.int32, (1, span), 1)
    for down in range(3):
        for other in range(cols):
            pair = gathered[down, other, : 2 * tile_rows].astype(jnp.float32)
            for image in range(2):
                lines[
                    image,
                    down * tile_rows : (down + 1) * tile_rows,
                    other * tile_cols : (other + 1) * tile_cols,
                ] = pair[image * tile_rows : (image + 1) * tile_rows]
    lines[:, :, cols * tile_cols :] = jnp.zeros((2, 3 * tile_rows, tile_cols), jnp.float32)

    def tower(image):
        current = jnp.concatenate(
            [
                lines[image, pl.ds(tile_rows + line - RIM + i, 1), :]
                for i in range(2 * RIM + 1)
            ],
            axis=1,
        )
        for num in range(RIM):
            edge = RIM - 1 - num
            inside = []
            for i in range(-edge, edge + 1):
                place = row * tile_rows + line + i
                limit = jnp.where((place >= 0) & (place < rows * tile_rows), cols * tile_cols, 0)
                inside.append(jnp.where(column < limit, 1.0, 0.0))
            inside = jnp.concatenate(inside, axis=1)
            current = layer(current, weights[num], span, 2 * edge + 1, num < RIM - 1, inside)
        return current

    left = tower(0)
    right = tower(1)
    ext = 2 * tile_cols
    flip = lax.broadcasted_iota(jnp.int32, (ext, ext), 0) + lax.broadcasted_iota(
        jnp.int32, (ext, ext), 1
    )
    flip = (flip == ext - 1).astype(jnp.float32).astype(jnp.bfloat16)
    shifts = lax.broadcasted_iota(jnp.int32, (tile_cols, NDISP), 1).astype(jnp.float32)
    for tile in range(cols):
        begin = tile * tile_cols
        own = left[:, begin : begin + tile_cols].T
        before = (begin or span) - tile_cols
        other = jnp.concatenate(
            [right[:, before : before + tile_cols], right[:, begin : begin + tile_cols]], axis=1
        )
        other = jnp.dot(other.astype(jnp.bfloat16), flip, preferred_element_type=jnp.float32)
        own_norm = jnp.maximum(jnp.sqrt(jnp.sum(own * own, axis=1, keepdims=True)), 1.0)
        other_norm = jnp.maximum(jnp.sqrt(jnp.sum(other * other, axis=0, keepdims=True)), 1.0)
        products = jnp.dot(
            own.astype(jnp.bfloat16),
            other.astype(jnp.bfloat16),
            preferred_element_type=jnp.float32,
        )
        cosine = products * (1.0 / own_norm) * (1.0 / other_norm)
        cosine = pltpu.roll(cosine, ext - tile_cols + 1, 1, stride=1, stride_axis=0)
        extent = gathered[1, tile, 2 * tile_rows :].astype(jnp.float32)
        base, width = extent[0:1], extent[tile_rows : tile_rows + 1]
        in_range = (shifts >= base) & (shifts < base + width)
        cost = jnp.where(in_range, 1.0 - cosine[:, :NDISP], INVALID_COST).astype(jnp.bfloat16)
        by_tile[tile] = cost
        cost = cost.astype(jnp.float32)
        for block in range(blocks):
            by_col[tile, :, block, :] = cost[block * STEPS : (block + 1) * STEPS]

    for tile in range(cols):

        @pl.when(leads & (col != tile))
        def _():
            volume_copy(tile, line, tile).start()

        @pl.when(leads & (col == tile))
        def _():
            volume[line] = by_tile[tile]

    sub = lax.broadcasted_iota(jnp.int32, vreg, 0)
    lane = lax.broadcasted_iota(jnp.int32, vreg, 1)
    first_edge = jnp.where(sub == 0, BIG_VALUE, PENALTY_SMALL)
    last_edge = jnp.where(sub == SUBS - 1, BIG_VALUE, PENALTY_SMALL)
    near_row = lax.broadcasted_iota(jnp.int32, (NDISP, NDISP), 0)
    near_col = lax.broadcasted_iota(jnp.int32, (NDISP, NDISP), 1)
    order = ((near_row % SUBS) * LEADS + near_row // SUBS == near_col).astype(jnp.float32)
    order = order.astype(jnp.bfloat16)
    same = (near_row == near_col).astype(jnp.float32).astype(jnp.bfloat16)

    def ordered(block):
        return lax.dot_general(
            order, block, (((1,), (1,)), ((), ())), preferred_element_type=jnp.float32
        )

    def upright(block, parts):
        return sum(
            lax.dot_general(
                same, part, (((1,), (1,)), ((), ())), preferred_element_type=jnp.float32
            )
            for part in split(block)[:parts]
        )

    def lay(ref, where, state):
        for lead in range(LEADS):
            ref[(*where, pl.ds(lead, SUBS, stride=LEADS), slice(None))] = state[lead]

    def put(ref, where, block):
        for lead in range(LEADS):
            ref[(*where, lead)] = block[lead * SUBS : lead * SUBS + SUBS]

    def take(ref, *where):
        return tuple(ref[(*where, lead)] for lead in range(LEADS))

    def advance(state, here):
        lowest = least(state)
        lowest = jnp.minimum(lowest, pltpu.roll(lowest, 4, 0))
        turned = [pltpu.roll(lowest, shift, 0) for shift in (1, 2, 3)]
        lowest = jnp.minimum(
            jnp.minimum(lowest, turned[0]), jnp.minimum(turned[1], turned[2])
        )
        jump = lowest + PENALTY_LARGE
        below = pltpu.roll(state[LEADS - 1], 1, 0) + first_edge
        above = pltpu.roll(state[0], SUBS - 1, 0) + last_edge
        ext = [below, *(value + PENALTY_SMALL for value in state), above]
        new = []
        for lead in range(LEADS):
            near = jnp.minimum(state[lead], jnp.minimum(ext[lead], ext[lead + 2]))
            new.append(jnp.minimum(near, jump) + here[lead])
        return tuple(new), lowest

    def slot_of(off):
        return 2 * STEPS if off == 0 else off + STEPS - (off > 0)

    for off in range(-STEPS, STEPS + 1):
        inside = (lane + off >= 0) & (lane + off < NDISP)
        outside[slot_of(off)] = jnp.where(inside, 0.0, BIG_VALUE)

    def transfer(way, tile):
        reached = {0: jnp.zeros(vreg, jnp.float32)}
        reach[way, tile, 0] = reached[0]
        for step in range(STEPS):
            here = by_col[tile, STEPS - 1 - step if way else step]
            after = {}
            for off in range(-step - 1, step + 2):
                cost = here
                if off:
                    cost = pltpu.roll(here, -off % NDISP, 1) + outside[slot_of(off)]
                side = [reached[o] for o in (off - 1, off + 1) if o in reached]
                near = least(side) + PENALTY_SMALL if side else None
                if off in reached:
                    near = reached[off] if near is None else jnp.minimum(reached[off], near)
                after[off] = near + cost
            reached = after
            if step < STEPS - 1:
                reach[way, tile, step + 1] = least(reached.values())
            else:
                for off, value in reached.items():
                    local[way, tile, slot_of(off)] = value
            yield

    def landings(group, works):
        def turn(step, carried):
            pieces = [
                by_col[group * SUBS : (group + 1) * SUBS, first].reshape(half, NDISP)
                for first in (step, STEPS - 1 - step)
            ]
            put(h_cost, (step,), ordered(jnp.concatenate(pieces, axis=0).astype(jnp.bfloat16)))
            return carried

        lax.fori_loop(0, STEPS, turn, 0, unroll=True)

        def pair(index, carried):
            start = 2 * index
            first = advance(take(h_cost, start), take(h_cost, start + 1))[0]
            second = take(h_cost, start + 1)

            def move(number, states):
                for step in (0, 1):
                    here = take(h_cost, 2 * number + step)
                    states = tuple(advance(state, here)[0] for state in states)
                return states

            states = lax.fori_loop(index + 1, STEPS // 2, move, (first, second))
            for num, state in enumerate(states):
                lay(turned, (start + num,), state)
            return carried

        if together:
            for index in range(STEPS // 2):
                pair(index, 0)
        else:
            lax.fori_loop(0, STEPS // 2, pair, 0)
        for start in range(STEPS):
            block = upright(turned[start], 3) + PENALTY_LARGE
            for way in range(2):
                value = block[way * half : way * half + half].reshape(SUBS, *vreg)
                landed[way, group * SUBS : (group + 1) * SUBS, start] = value
            for work in works:
                next(work)

    together = cols <= SUBS
    works = [transfer(0, 0), transfer(1, cols - 1)] if together else []
    for group in range(groups):
        landings(group, works)

    if not together:

        def one_tile(tile, carried):
            for way in range(2):
                for _ in transfer(way, tile):
                    pass
            return carried

        lax.fori_loop(0, cols, one_tile, 0)

    def v_turn(turn):
        lower_half = row > rows - 1 - row
        backward = lower_half != (turn == 1)
        way = backward.astype(jnp.int32)
        step = 1 - 2 * way
        has_source = (row - step >= 0) & (row - step < rows)
        has_target = (row + step >= 0) & (row + step < rows)
        copy = pltpu.make_async_remote_copy(
            src_ref=v_send.at[way],
            dst_ref=v_recv.at[way],
            send_sem=v_send_sem.at[way],
            recv_sem=v_recv_sem.at[way],
            device_id={"row": row + step},
            device_id_type=MESH,
        )
        return copy, has_source, has_target, way, backward

    def column_sweep(turn):
        copy, has_source, has_target, way, backward = v_turn(turn)

        @pl.when(has_source)
        def _():
            copy.wait_recv()

        @pl.when(jnp.logical_not(has_source))
        def _():
            v_recv[way] = jnp.zeros(v_recv.shape[1:], jnp.float32)

        def body(index, state):
            place = jnp.where(backward, tile_rows - 1 - index, index)
            state, lowest = advance(state, take(v_cost, place))
            state = tuple(value - lowest for value in state)
            lay(v_path, (way, place), state)
            return state

        state = lax.fori_loop(0, tile_rows, body, take(v_recv, way), unroll=4)
        for lead in range(LEADS):
            v_send[way, lead] = state[lead]

        @pl.when(has_target)
        def _():
            copy.start()

    def vertical(point):
        outer = jnp.minimum(row, rows - 1 - row)
        for turn, stage in enumerate((outer, rows - 1 - outer)):

            @pl.when(stage * 4 // rows == point)
            def _():
                column_sweep(turn)

    def entry_copy(way, tile, y, target):
        return pltpu.make_async_remote_copy(
            src_ref=entry_out.at[way, tile],
            dst_ref=entry_in.at[way, y],
            send_sem=entry_send_sem.at[way, tile],
            recv_sem=entry_recv_sem.at[way, y],
            device_id={"col": target},
            device_id_type=MESH,
        )

    def everywhere(value):
        for shift in (4, 2, 1):
            value = jnp.minimum(value, pltpu.roll(value, shift, 0))
        return value

    def cross(way, tile, block, state):
        lows, best = [], None
        for part in range(0, STEPS, SUBS):
            where = pl.ds(part, SUBS)
            gone = state + reach[way, tile, where, block, :]
            low = jnp.broadcast_to(jnp.min(gone, axis=1, keepdims=True), vreg)
            landing = low + landed[way, tile, where, block, :]
            lows.append(low)
            best = landing if best is None else jnp.minimum(best, landing)
        still = local[way, tile, pl.ds(2 * STEPS, 1), block, :]
        best = jnp.minimum(best, state + still)
        for part in range(0, 2 * STEPS, SUBS):
            moved = state + local[way, tile, pl.ds(part, SUBS), block, :]
            off = part - STEPS + (part >= STEPS)
            moved = pltpu.roll(moved, off % NDISP, 1, stride=1, stride_axis=0)
            best = jnp.minimum(best, moved)
        return everywhere(best) - everywhere(lows[0])

    def tile_wait():
        for y in range(tile_rows):

            @pl.when(col != y * share)
            def _():
                volume_copy(y, y, col).wait_recv()

    def tile_line(y):
        put(v_cost, (y,), ordered(volume[y]))

    def tile_turns():
        for y in range(tile_rows):
            wide[y] = volume[y].astype(jnp.float32)
        def tile_turn(step, carried):
            pieces = [
                wide[y, pl.ds(first, blocks, stride=STEPS), :]
                for first in (step, STEPS - 1 - step)
                for y in range(tile_rows)
            ]
            put(t_cost, (step,), ordered(jnp.concatenate(pieces, axis=0).astype(jnp.bfloat16)))
            return carried

        lax.fori_loop(0, STEPS, tile_turn, 0, unroll=True)

    states = (jnp.zeros(vreg, jnp.float32),) * 2
    point = 0
    for number in range(cols):
        tiles = (number, cols - 1 - number)

        def one_block(index, states):
            after = []
            for way in range(2):
                block = blocks - 1 - index if way else index
                entry_out[way, tiles[way], pl.ds(block, 1), :] = states[way][0:1]
                after.append(cross(way, tiles[way], block, states[way]))
            return tuple(after)

        if together:
            ahead = []
            if number < cols - 1:
                ahead = [transfer(0, number + 1), transfer(1, cols - 2 - number)]
            for index in range(blocks):
                states = one_block(index, states)
                for _ in range(len(ahead) * STEPS // blocks):
                    next(ahead[index * 2 // blocks])
                if number == 3 * cols // 8:
                    tile_line(index)
        else:
            states = lax.fori_loop(0, blocks, one_block, states)
        for way in range(2):
            tile = tiles[way]

            @pl.when(leads & (col != tile))
            def _():
                entry_copy(way, tile, line, tile).start()

            @pl.when(leads & (col == tile))
            def _():
                entry_in[way, line] = entry_out[way, tile]

        if number == 3 * cols // 8 - 1:
            tile_wait()
        if number == 3 * cols // 8 and not together:
            for y in range(tile_rows):
                tile_line(y)
        while point < 3 and number == POINTS[point] * cols // 8 - 1:
            vertical(point)
            point += 1

    tile_turns()
    vertical(3)
    for y in range(tile_rows):
        total[y] = upright(v_path[0, y] + v_path[1, y], 2)

    for y in range(tile_rows):
        for way in range(2):

            @pl.when(col != y * share)
            def _():
                entry_copy(way, y, y, col).wait_recv()

    block = entry_in[...].reshape(NDISP, NDISP)
    block = sum(ordered(part) for part in split(block))
    state = tuple(block[lead * SUBS : lead * SUBS + SUBS] for lead in range(LEADS))

    def dense(index, state):
        state, lowest = advance(state, take(t_cost, index))
        state = tuple(value - lowest for value in state)
        lay(h_path, (index,), state)
        return state

    lax.fori_loop(0, STEPS, dense, state, unroll=True)

    def gather_step(step, carried):
        block = upright(h_path[step], 2)
        for way in range(2):
            where = pl.ds(STEPS - 1 - step if way else step, blocks, stride=STEPS)
            for y in range(tile_rows):
                begin = way * half + y * blocks
                total[y, where, :] = total[y, where, :] + block[begin : begin + blocks]
        return carried

    lax.fori_loop(0, STEPS, gather_step, 0, unroll=True)
    for y in range(tile_rows):
        out_ref[y] = (total[y] * 0.25).astype(jnp.bfloat16)

    for tile in range(cols):

        @pl.when(leads & (col != tile))
        def _():
            volume_copy(tile, line, tile).wait_send()
            for way in range(2):
                entry_copy(way, tile, line, tile).wait_send()

    for turn in range(2):
        copy, _, has_target, _, _ = v_turn(turn)

        @pl.when(has_target)
        def _():
            copy.wait_send()

    for down, other, k in moves:

        @pl.when(sends(down, other))
        def _():
            image_copy(down, other, col, k).wait_send()


def aggregate(tile_base, tile_width, *arrays):
    tile_rows, tile_cols = arrays[0].shape
    cols = lax.axis_size("col")
    vreg = (SUBS, NDISP)
    vregs = (LEADS, *vreg)
    blocks = tile_cols // STEPS
    tile = (tile_rows, tile_cols, NDISP)
    fields = (FIELDS * tile_rows, tile_cols)
    return pl.pallas_call(
        partial(path_kernel, tile_rows, tile_cols),
        out_shape=pltpu.VMEM(tile, jnp.bfloat16),
        in_specs=[pl.BlockSpec(memory_space=pltpu.SMEM)] * 2
        + [pl.BlockSpec(memory_space=pltpu.HBM)] * 5,
        out_specs=pl.BlockSpec(memory_space=pltpu.VMEM),
        scratch_shapes=[
            *(pltpu.VMEM(array.shape, array.dtype) for array in arrays),
            pltpu.VMEM(fields, jnp.bfloat16),
            pltpu.VMEM((3, cols, *fields), jnp.bfloat16),
            pltpu.VMEM((2, 3 * tile_rows, (cols + 1) * tile_cols), jnp.float32),
            pltpu.VMEM((cols, STEPS, blocks, NDISP), jnp.float32),
            pltpu.VMEM((cols, tile_cols, NDISP), jnp.bfloat16),
            pltpu.VMEM(tile, jnp.bfloat16),
            pltpu.VMEM(tile, jnp.float32),
            pltpu.VMEM((tile_rows, *vregs), jnp.float32),
            pltpu.VMEM((STEPS, *vregs), jnp.float32),
            pltpu.VMEM((STEPS, *vregs), jnp.float32),
            pltpu.VMEM((2, tile_rows, NDISP, NDISP), jnp.float32),
            pltpu.VMEM((STEPS, NDISP, NDISP), jnp.float32),
            pltpu.VMEM((STEPS, NDISP, NDISP), jnp.float32),
            pltpu.VMEM(tile, jnp.float32),
            pltpu.VMEM((2 * STEPS + 1, *vreg), jnp.float32),
            pltpu.VMEM((2, cols, 2 * STEPS + 1, *vreg), jnp.float32),
            pltpu.VMEM((2, cols, STEPS, *vreg), jnp.float32),
            pltpu.VMEM((2, cols, STEPS, *vreg), jnp.float32),
            pltpu.VMEM((2, cols, blocks, NDISP), jnp.float32),
            pltpu.VMEM((2, tile_rows, blocks, NDISP), jnp.float32),
            pltpu.VMEM((2, *vregs), jnp.float32),
            pltpu.VMEM((2, *vregs), jnp.float32),
            pltpu.SemaphoreType.DMA((3, cols)),
            pltpu.SemaphoreType.DMA((3, cols)),
            pltpu.SemaphoreType.DMA((cols,)),
            pltpu.SemaphoreType.DMA((tile_rows,)),
            pltpu.SemaphoreType.DMA((2, cols)),
            pltpu.SemaphoreType.DMA((2, tile_rows)),
            pltpu.SemaphoreType.DMA((2,)),
            pltpu.SemaphoreType.DMA((2,)),
            pltpu.SemaphoreType.DMA((len(arrays),)),
        ],
        compiler_params=pltpu.CompilerParams(
            collective_id=0, has_side_effects=True, vmem_limit_bytes=56 << 20
        ),
        name="paths",
    )(tile_base, tile_width, *arrays)


def on_device(
    left_image, right_image, first_weight, second_weight, third_weight, tile_base, tile_width
):
    return aggregate(
        tile_base, tile_width, left_image, right_image, first_weight.T, second_weight, third_weight
    )


def solution(mesh):
    placed = (P("row", "col"), P("row", "col"), P(), P(), P(), P("row", "col"), P("row", "col"))
    return jax.shard_map(
        on_device, mesh=mesh, in_specs=placed, out_specs=P("row", "col", None), check_vma=False
    )
```
